32 devices in a mesh: groups: 2 (over x), blk: 16 (over z, y, core).
Axes of the slice: x: 2, y: 2, z: 4, core: 2. Of those that a mesh axis runs over, the one named last changes fastest.
Arguments:
- activations: bfloat16 [4096, 8192], P(('groups', 'blk')), parts along dimension 0, may hold values from -6 to 6
- out_grad: bfloat16 [4096, 8192], P(('groups', 'blk')), parts along dimension 0, may hold values from -0.59765625 to 0.59765625
- down_panels: bfloat16 [256, 32, 8192], P('blk'), may hold values from -0.0625 to 0.0625
- up_panels: bfloat16 [256, 32, 8192], P('blk'), may hold values from -0.0625 to 0.0625
- routes: int32 [32, 2], P(('groups', 'blk')), parts along dimension 0, may hold values from 0 to 255, as said below
- gates: float32 [32, 2], P(('groups', 'blk')), parts along dimension 0, may hold values from 0.25 to 1
Outputs:
- down_grad: bfloat16 [512, 32, 8192], P(('groups', 'blk')), parts along dimension 0
- up_grad: bfloat16 [512, 32, 8192], P(('groups', 'blk')), parts along dimension 0
The draws below stay inside these ranges and needn't reach their ends.
There are 2 independent parts, one for each index of `groups`. The reference program is written for one: setup_inputs(seed, part) draws one part's arguments, and reference() takes and returns one part's arrays. A program takes and returns all parts, laid end to end along the dimension named above; an argument that names none is the same for every part. Nothing has to cross between parts.
Inputs may be any that keep to these rules, and one draw needn't show every extreme that they name: `routes`: each block names two different adapters.
All inputs are finite; a program needn't handle non-finite values.
Results may differ from the reference program's by a relative error of at most 0.005.
Values may be sent and summed in bfloat16 or wider, within the bound.
No kernel may reach another device: no remote copies, remote signals or barrier semaphores. Data moves between devices by JAX's collectives and lax.ppermute only.
A program may use at most 192 MiB of HBM per device.

```python
import jax
import jax.numpy as jnp

D = 8192
R = 32
E = 256
BLK = 128
BLOCKS = 16
TOKENS = 2048


def draw_routes(key, part):
    first_key = jax.random.fold_in(key, 11)
    second_key = jax.random.fold_in(key, 12)
    first = jax.random.randint(first_key, (BLOCKS,), 0, E, dtype=jnp.int32)
    offset = jax.random.randint(second_key, (BLOCKS,), 1, E, dtype=jnp.int32)
    first = first.at[0].set(E - 1)
    offset = offset.at[0].set(1)
    second = (first + offset) % E
    return jnp.stack([first, second], axis=1).astype(jnp.int32)


def block_scale(key, dims, shards, low, largest):
    level, own = 1.0, jax.random.fold_in(key, 6)
    for dim, shards_of in shards:
        heights = jnp.exp(jax.random.uniform(jax.random.fold_in(own, dim), (shards_of,), jnp.float32, low / len(shards), largest / len(shards)))
        level = level * jnp.repeat(heights, dims[dim] // shards_of).reshape([-1 if axis == dim else 1 for axis in range(len(dims))])
    return level


def centred(stream_key, dims, width, most, cuts=(), held_as=jnp.bfloat16):
    array = jax.random.normal(stream_key, dims, jnp.float32) * width
    if len(cuts) > 0:
        array = block_scale(stream_key, dims, cuts, -0.22, 0.18) * array
    return jnp.clip(array, min=-most, max=most).astype(held_as)


def setup_inputs(seed: int = 0, part: int = 0) -> dict:
    seeds = jax.random.split(jax.random.key(seed), 7)
    part_keys = jax.random.split(jax.random.fold_in(seeds[6], part), 7)
    return {
        "activations": centred(part_keys[0], (TOKENS, D), 1.0, 6.0, ((0, 16),)),
        "out_grad": centred(part_keys[1], (TOKENS, D), 0.1, 0.59765625, ((0, 16),)),
        "down_panels": centred(seeds[2], (E, R, D), D ** -0.5, 0.0625, ((0, 16),)),
        "up_panels": centred(seeds[3], (E, R, D), D ** -0.5, 0.0625, ((0, 16),)),
        "routes": draw_routes(jax.random.fold_in(jax.random.fold_in(seeds[6], part), 71), part),
        "gates": jnp.clip(0.25 + 0.75 * jax.random.uniform(part_keys[5], (BLOCKS, 2), jnp.float32) ** block_scale(part_keys[5], (BLOCKS, 2), ((0, 16),), -0.2, 0.2), 0.25, 1.0),
    }


def reference(activations, out_grad, down_panels, up_panels, routes, gates):
    rows = activations.reshape(BLOCKS, BLK, D).astype(jnp.float32)
    grads = out_grad.reshape(BLOCKS, BLK, D).astype(jnp.float32)
    down_sel = down_panels[routes].astype(jnp.float32)
    up_sel = up_panels[routes].astype(jnp.float32)
    low = jnp.einsum('btd,bkrd->bkrt', rows, down_sel).astype(jnp.bfloat16)
    back = jnp.einsum('btd,bkrd->bkrt', grads, up_sel).astype(jnp.bfloat16)
    weights = gates.astype(jnp.float32)[:, :, None, None]
    up_terms = jnp.einsum('bkrt,btd->bkrd', low.astype(jnp.float32), grads) * weights
    down_terms = jnp.einsum('bkrt,btd->bkrd', back.astype(jnp.float32), rows) * weights
    flat = routes.reshape(-1).astype(jnp.int32)
    up_grad = jax.ops.segment_sum(up_terms.reshape(BLOCKS * 2, R, D), flat, E)
    down_grad = jax.ops.segment_sum(down_terms.reshape(BLOCKS * 2, R, D), flat, E)
    return down_grad.astype(jnp.bfloat16), up_grad.astype(jnp.bfloat16)
```

```python
import functools

import jax
import jax.numpy as jnp
from jax import lax
from jax.experimental import pallas as pl
from jax.experimental.pallas import tpu as pltpu
from jax.sharding import PartitionSpec as P

ANY = pl.BlockSpec(memory_space=pl.ANY)
SMEM = pl.BlockSpec(memory_space=pltpu.SMEM)
VMEM = pl.BlockSpec(memory_space=pltpu.VMEM)
CAPACITIES = (6, 7, 8, 10)


def tables_kernel(groups, blocks, held, where_ref, routes_ref, src_ref, slot_ref, first_ref, count_ref, final_ref, most_ref, seen, load):
    requests = 2 * blocks
    chips = blocks // 2
    group, me = where_ref[0], where_ref[1]
    chip = me // 2

    def clear(ref, n, value):
        def body(i, _):
            ref[i] = value
            return 0

        lax.fori_loop(0, n, body, 0)

    clear(src_ref, 2 * held, -1)
    clear(final_ref, held, -1)
    clear(count_ref, requests, 0)

    def scan(which, most, mine):
        base = which * requests
        clear(load, chips, 0)

        def unsee(i, _):
            seen[routes_ref[base + i]] = -1
            return 0

        lax.fori_loop(0, requests, unsee, 0)

        def visit(i, most):
            adapter = routes_ref[base + i]
            before = seen[adapter]
            new = before < 0
            owner = adapter // (2 * held)
            rank = load[owner]

            @pl.when(new)
            def _():
                seen[adapter] = i
                load[owner] = rank + 1

            if mine:
                first = jnp.where(new, i, before)
                first_ref[i] = first
                count_ref[first] = count_ref[first] + 1

                @pl.when(new)
                def _():
                    slot_ref[2 * i] = owner
                    slot_ref[2 * i + 1] = rank

                @pl.when(jnp.logical_not(new))
                def _():
                    slot_ref[2 * i] = slot_ref[2 * before]
                    slot_ref[2 * i + 1] = slot_ref[2 * before + 1]

                @pl.when(new & (owner == chip))
                def _():
                    src_ref[rank] = adapter - owner * (2 * held)

                @pl.when(new & (adapter // held == me))
                def _():
                    final_ref[adapter - me * held] = rank

            return jnp.maximum(most, rank + new.astype(jnp.int32))

        return lax.fori_loop(0, requests, visit, most)

    most = scan(group, jnp.int32(0), True)
    most_ref[0] = lax.fori_loop(0, groups, lambda g, m: scan(g, m, False), most)


def hand_over_kernel(cap, held, where_ref, src_ref, down_ref, up_ref, out_ref, sems):
    rank, width = down_ref.shape[1], down_ref.shape[2]
    half = width // 2
    core = where_ref[1] % 2
    columns = pl.ds(pl.multiple_of((1 - core) * half, 128), half)

    def copies(c):
        a = src_ref[c] - core * held
        return (
            pltpu.make_async_copy(down_ref.at[a, :, columns], out_ref.at[c, pl.ds(0, rank)], sems.at[2 * c]),
            pltpu.make_async_copy(up_ref.at[a, :, columns], out_ref.at[c, pl.ds(rank, rank)], sems.at[2 * c + 1]),
        )

    def each(act):
        for c in range(cap):
            a = src_ref[c] - core * held

            @pl.when((src_ref[c] >= 0) & (a >= 0) & (a < held))
            def _(c=c):
                for copy in copies(c):
                    act(copy)

    each(lambda copy: copy.start())
    each(lambda copy: copy.wait())


def compose_kernel(held, chips, where_ref, src_ref, down_ref, up_ref, other_ref, out_ref):
    rank = down_ref.shape[1]
    part = out_ref.shape[3]
    core = where_ref[1] % 2
    adapter = src_ref[pl.program_id(0)]
    mine = (adapter >= 0) & (adapter // held == core)

    @pl.when(mine)
    def _():
        for p in range(chips):
            out_ref[p, 0, :rank, :] = down_ref[0, :, p * part : (p + 1) * part]
            out_ref[p, 0, rank:, :] = up_ref[0, :, p * part : (p + 1) * part]

    @pl.when(jnp.logical_not(mine))
    def _():
        for p in range(chips):
            out_ref[p, 0] = other_ref[0, :, p * part : (p + 1) * part]


def pick_kernel(cap, slot_ref, held_ref, out_ref, sems):
    requests = out_ref.shape[0]

    def copy(i):
        s = slot_ref[2 * i] * cap + slot_ref[2 * i + 1]
        return pltpu.make_async_copy(held_ref.at[s], out_ref.at[i], sems.at[i])

    def start(i, _):
        copy(i).start()
        return 0

    def wait(i, _):
        copy(i).wait()
        return 0

    lax.fori_loop(0, requests, start, 0)
    lax.fori_loop(0, requests, wait, 0)


def terms_kernel(gates_ref, rows_ref, grads_ref, panels_ref, out_ref):
    devices, slots, double, part = panels_ref.shape
    rank = double // 2
    tokens, width = rows_ref.shape
    last = (((1,), (1,)), ((), ()))

    def columns(d):
        return pl.ds(pl.multiple_of((d % 2) * (width // 2) + (d // 2) * part, 128), part)

    def gather(d, sums):
        low, back = sums
        cols = columns(d)
        down = panels_ref[d, :, :rank, :].reshape(slots * rank, part)
        up = panels_ref[d, :, rank:, :].reshape(slots * rank, part)
        low += lax.dot_general(down, rows_ref[:, cols], last, preferred_element_type=jnp.float32)
        back += lax.dot_general(up, grads_ref[:, cols], last, preferred_element_type=jnp.float32)
        return low, back

    zero = jnp.zeros((slots * rank, tokens), jnp.float32)
    low, back = lax.fori_loop(0, devices, gather, (zero, zero), unroll=4)
    low, back = low.astype(jnp.bfloat16), back.astype(jnp.bfloat16)

    def spread(d, _):
        cols = columns(d)
        up = jnp.dot(low, grads_ref[:, cols], preferred_element_type=jnp.float32)
        down = jnp.dot(back, rows_ref[:, cols], preferred_element_type=jnp.float32)
        for k in range(slots):
            gate = gates_ref[0, k]
            out_ref[d, k, :rank, :] = (down[k * rank : (k + 1) * rank] * gate).astype(out_ref.dtype)
            out_ref[d, k, rank:, :] = (up[k * rank : (k + 1) * rank] * gate).astype(out_ref.dtype)
        return 0

    lax.fori_loop(0, devices, spread, 0, unroll=4)


def merge_kernel(cap, slot_ref, first_ref, count_ref, terms_ref, out_ref, total):
    requests = terms_ref.shape[0]

    def visit(i, _):
        s = slot_ref[2 * i] * cap + slot_ref[2 * i + 1]

        @pl.when((first_ref[i] == i) & (count_ref[i] == 1))
        def _():
            out_ref[s] = terms_ref[i]

        @pl.when((first_ref[i] == i) & (count_ref[i] > 1))
        def _():
            total[...] = terms_ref[i].astype(jnp.float32)

            def add(j, _):
                @pl.when(first_ref[j] == i)
                def _():
                    total[...] += terms_ref[j].astype(jnp.float32)

                return 0

            lax.fori_loop(i + 1, requests, add, 0)
            out_ref[s] = total[...].astype(out_ref.dtype)

        return 0

    lax.fori_loop(0, requests, visit, 0)


def home_kernel(chips, where_ref, final_ref, own_ref, other_ref, down_ref, up_ref):
    rank, width = down_ref.shape[1], down_ref.shape[2]
    part = own_ref.shape[3]
    core = where_ref[1] % 2
    slot = final_ref[pl.program_id(0)]

    @pl.when(slot >= 0)
    def _():
        for side, ref in ((core, own_ref), (1 - core, other_ref)):
            for p in range(chips):
                cols = pl.ds(pl.multiple_of(side * (width // 2) + p * part, 128), part)
                down_ref[0, :, cols] = ref[p, 0, :rank, :]
                up_ref[0, :, cols] = ref[p, 0, rank:, :]

    @pl.when(slot < 0)
    def _():
        down_ref[...] = jnp.zeros_like(down_ref)
        up_ref[...] = jnp.zeros_like(up_ref)


def with_capacity(cap, blocks, where, src, slot, first, count, final, activations, out_grad, down_panels, up_panels, gates):
    held, rank, width = down_panels.shape
    chips = blocks // 2
    half = width // 2
    part = width // blocks
    bf16 = jnp.bfloat16
    partner = [(i, i ^ 1) for i in range(blocks)]
    same_core = [[2 * i + c for i in range(chips)] for c in range(2)]

    send = pl.pallas_call(
        functools.partial(hand_over_kernel, cap, held),
        out_shape=jax.ShapeDtypeStruct((cap, 2 * rank, half), bf16),
        in_specs=[SMEM, SMEM, ANY, ANY],
        out_specs=ANY,
        scratch_shapes=[pltpu.SemaphoreType.DMA((2 * cap,))],
        name="hand_over",
    )(where, src, down_panels, up_panels)
    other = lax.ppermute(send, "blk", partner)

    def panel_index(c, where_ref, src_ref):
        a = src_ref[c] - (where_ref[1] % 2) * held
        return (jnp.where((a >= 0) & (a < held), a, 0), 0, where_ref[1] % 2)

    slices = pl.pallas_call(
        functools.partial(compose_kernel, held, chips),
        out_shape=jax.ShapeDtypeStruct((chips, cap, 2 * rank, part), bf16),
        grid_spec=pltpu.PrefetchScalarGridSpec(
            num_scalar_prefetch=2,
            grid=(cap,),
            in_specs=[
                pl.BlockSpec((1, rank, half), panel_index),
                pl.BlockSpec((1, rank, half), panel_index),
                pl.BlockSpec((1, 2 * rank, half), lambda c, w, s: (c, 0, 0)),
            ],
            out_specs=pl.BlockSpec((chips, 1, 2 * rank, part), lambda c, w, s: (0, c, 0, 0)),
        ),
        name="compose",
    )(where, src, down_panels, up_panels, other)
    slices = lax.all_to_all(slices, "blk", 0, 0, tiled=True, axis_index_groups=same_core)

    picked = pl.pallas_call(
        functools.partial(pick_kernel, cap),
        out_shape=jax.ShapeDtypeStruct((2 * blocks, 2 * rank, part), bf16),
        in_specs=[SMEM, ANY],
        out_specs=ANY,
        scratch_shapes=[pltpu.SemaphoreType.DMA((2 * blocks,))],
        name="pick",
    )(slot, slices.reshape(chips * cap, 2 * rank, part))
    panels = lax.all_to_all(picked.reshape(blocks, 2, 2 * rank, part), "blk", 0, 0, tiled=True)

    terms = pl.pallas_call(
        terms_kernel,
        out_shape=jax.ShapeDtypeStruct((blocks, 2, 2 * rank, part), bf16),
        in_specs=[SMEM, VMEM, VMEM, VMEM],
        out_specs=VMEM,
        name="terms",
    )(gates, activations, out_grad, panels)
    terms = lax.all_to_all(terms, "blk", 0, 0, tiled=True)

    sums = pl.pallas_call(
        functools.partial(merge_kernel, cap),
        out_shape=jax.ShapeDtypeStruct((chips * cap, 2 * rank, part), bf16),
        in_specs=[SMEM, SMEM, SMEM, VMEM],
        out_specs=VMEM,
        scratch_shapes=[pltpu.VMEM((2 * rank, part), jnp.float32)],
        name="merge",
    )(slot, first, count, terms.reshape(2 * blocks, 2 * rank, part))
    own = lax.all_to_all(sums.reshape(chips, cap, 2 * rank, part), "blk", 0, 0, tiled=True, axis_index_groups=same_core)
    other = lax.ppermute(own, "blk", partner)

    def slot_index(a, where_ref, final_ref):
        return (0, jnp.maximum(final_ref[a], 0), 0, 0)

    shape = jax.ShapeDtypeStruct((held, rank, width), bf16)
    return pl.pallas_call(
        functools.partial(home_kernel, chips),
        out_shape=(shape, shape),
        grid_spec=pltpu.PrefetchScalarGridSpec(
            num_scalar_prefetch=2,
            grid=(held,),
            in_specs=[pl.BlockSpec((chips, 1, 2 * rank, part), slot_index)] * 2,
            out_specs=[pl.BlockSpec((1, rank, width), lambda a, w, f: (a, 0, 0))] * 2,
        ),
        name="home",
    )(where, final, own, other)


def shards(groups, blocks, activations, out_grad, down_panels, up_panels, routes, gates):
    held = down_panels.shape[0]
    chips = blocks // 2
    where = jnp.stack([lax.axis_index("groups"), lax.axis_index("blk")]).astype(jnp.int32)
    copies = jnp.broadcast_to(routes.reshape(1, 1, 2), (groups * blocks, 1, 2))
    routes_all = lax.all_to_all(copies, ("groups", "blk"), 0, 0, tiled=True).reshape(-1)
    requests = 2 * blocks
    sizes = (2 * held, 2 * requests, requests, requests, held, 1)
    src, slot, first, count, final, most = pl.pallas_call(
        functools.partial(tables_kernel, groups, blocks, held),
        out_shape=tuple(jax.ShapeDtypeStruct((n,), jnp.int32) for n in sizes),
        in_specs=[SMEM, SMEM],
        out_specs=(SMEM,) * 6,
        scratch_shapes=[pltpu.SMEM((blocks * held,), jnp.int32), pltpu.SMEM((chips,), jnp.int32)],
        name="tables",
    )(where, routes_all)
    caps = [c for c in CAPACITIES if c < 2 * held] + [2 * held]
    branch = sum((most[0] > c).astype(jnp.int32) for c in caps[:-1])
    return lax.switch(
        branch,
        [functools.partial(with_capacity, c, blocks) for c in caps],
        where, src, slot, first, count, final, activations, out_grad, down_panels, up_panels, gates,
    )


def solution(mesh):
    in_specs = (
        P(("groups", "blk"), None),
        P(("groups", "blk"), None),
        P("blk", None, None),
        P("blk", None, None),
        P(("groups", "blk"), None),
        P(("groups", "blk"), None),
    )
    out_specs = (P(("groups", "blk"), None, None), P(("groups", "blk"), None, None))
    body = functools.partial(shards, mesh.shape["groups"], mesh.shape["blk"])
    return jax.shard_map(body, mesh=mesh, in_specs=in_specs, out_specs=out_specs, check_vma=False)
```

```python
import functools

import jax
import jax.numpy as jnp
from jax import lax
from jax.experimental import pallas as pl
from jax.experimental.pallas import tpu as pltpu
from jax.sharding import PartitionSpec as P

ANY = pl.BlockSpec(memory_space=pl.ANY)
SMEM = pl.BlockSpec(memory_space=pltpu.SMEM)
VMEM = pl.BlockSpec(memory_space=pltpu.VMEM)
CAPACITIES = (6, 7, 8, 9, 10)


def tables_kernel(groups, blocks, held, where_ref, routes_ref, src_ref, slot_ref, first_ref, count_ref, final_ref, most_ref, seen, load):
    requests = 2 * blocks
    chips = blocks // 2
    group, me = where_ref[0], where_ref[1]
    chip = me // 2

    def clear(ref, n, value):
        def body(i, _):
            ref[i] = value
            return 0

        lax.fori_loop(0, n, body, 0)

    clear(src_ref, 2 * held, -1)
    clear(final_ref, held, -1)
    clear(count_ref, requests, 0)

    def scan(which, most, mine):
        base = which * requests
        clear(load, chips, 0)

        def unsee(i, _):
            seen[routes_ref[base + i]] = -1
            return 0

        lax.fori_loop(0, requests, unsee, 0)

        def visit(i, most):
            adapter = routes_ref[base + i]
            before = seen[adapter]
            new = before < 0
            owner = adapter // (2 * held)
            rank = load[owner]

            @pl.when(new)
            def _():
                seen[adapter] = i
                load[owner] = rank + 1

            if mine:
                first = jnp.where(new, i, before)
                first_ref[i] = first
                count_ref[first] = count_ref[first] + 1

                @pl.when(new)
                def _():
                    slot_ref[2 * i] = owner
                    slot_ref[2 * i + 1] = rank

                @pl.when(jnp.logical_not(new))
                def _():
                    slot_ref[2 * i] = slot_ref[2 * before]
                    slot_ref[2 * i + 1] = slot_ref[2 * before + 1]

                @pl.when(new & (owner == chip))
                def _():
                    src_ref[rank] = adapter - owner * (2 * held)

                @pl.when(new & (adapter // held == me))
                def _():
                    final_ref[adapter - me * held] = rank

            return jnp.maximum(most, rank + new.astype(jnp.int32))

        return lax.fori_loop(0, requests, visit, most)

    most = scan(group, jnp.int32(0), True)
    most_ref[0] = lax.fori_loop(0, groups, lambda g, m: scan(g, m, False), most)


def repeat(n, body):
    def step(i, carry):
        body(i)
        return carry

    lax.fori_loop(0, n, step, 0)


def compose_kernel(cap, held, chips, where_ref, src_ref, down_ref, up_ref, far_down_ref, far_up_ref, out_ref, sems):
    part = out_ref.shape[3]
    core = where_ref[1] % 2

    def each(act):
        def visit(c):
            adapter = src_ref[c]
            near = adapter // held == core
            a = lax.rem(adapter, held)
            for kind, sources in ((0, (far_down_ref, down_ref)), (1, (far_up_ref, up_ref))):
                for own in (0, 1):

                    @pl.when((adapter >= 0) & (core == kind) & (near == (own == 1)))
                    def _(ref=sources[own]):
                        for p in range(chips):
                            act(pltpu.make_async_copy(ref.at[a, :, pl.ds(p * part, part)], out_ref.at[p, c], sems.at[c, p]))

        repeat(cap, visit)

    each(lambda copy: copy.start())
    each(lambda copy: copy.wait())


def pick_kernel(cap, slot_ref, held_ref, out_ref, sems):
    def copy(i):
        s = slot_ref[2 * i] * cap + slot_ref[2 * i + 1]
        return pltpu.make_async_copy(held_ref.at[s], out_ref.at[i], sems.at[i])

    requests = out_ref.shape[0]
    repeat(requests, lambda i: copy(i).start())
    repeat(requests, lambda i: copy(i).wait())


def terms_kernel(gates_ref, rows_ref, grads_ref, panels_ref, out_ref):
    devices, slots, rank, part = panels_ref.shape
    tokens = rows_ref.shape[0]
    chips = devices // 2
    last = (((1,), (1,)), ((), ()))

    def columns(p):
        return pl.ds(pl.multiple_of(p * part, 128), part)

    def gather(p, sums):
        low, back = sums
        cols = columns(p)
        down = panels_ref[2 * p].reshape(slots * rank, part)
        up = panels_ref[2 * p + 1].reshape(slots * rank, part)
        low += lax.dot_general(down, rows_ref[:, cols], last, preferred_element_type=jnp.float32)
        back += lax.dot_general(up, grads_ref[:, cols], last, preferred_element_type=jnp.float32)
        return low, back

    zero = jnp.zeros((slots * rank, tokens), jnp.float32)
    low, back = lax.fori_loop(0, chips, gather, (zero, zero), unroll=2)
    low, back = low.astype(jnp.bfloat16), back.astype(jnp.bfloat16)

    def spread(p, _):
        cols = columns(p)
        down = jnp.dot(back, rows_ref[:, cols], preferred_element_type=jnp.float32)
        up = jnp.dot(low, grads_ref[:, cols], preferred_element_type=jnp.float32)
        for k in range(slots):
            gate = gates_ref[0, k]
            out_ref[2 * p, k] = (down[k * rank : (k + 1) * rank] * gate).astype(out_ref.dtype)
            out_ref[2 * p + 1, k] = (up[k * rank : (k + 1) * rank] * gate).astype(out_ref.dtype)
        return 0

    lax.fori_loop(0, chips, spread, 0, unroll=2)


def merge_kernel(cap, slot_ref, first_ref, count_ref, terms_ref, out_ref, total, term, sems, sem):
    requests = terms_ref.shape[0]

    def slot(i):
        return slot_ref[2 * i] * cap + slot_ref[2 * i + 1]

    def each(act):
        def visit(i):
            @pl.when(first_ref[i] == i)
            def _():
                act(pltpu.make_async_copy(terms_ref.at[i], out_ref.at[slot(i)], sems.at[i]))

        repeat(requests, visit)

    each(lambda copy: copy.start())
    each(lambda copy: copy.wait())

    def visit(i):
        @pl.when((first_ref[i] == i) & (count_ref[i] > 1))
        def _():
            s = slot(i)
            total[...] = out_ref[s].astype(jnp.float32)

            def add(j):
                @pl.when((j > i) & (first_ref[j] == i))
                def _():
                    copy = pltpu.make_async_copy(terms_ref.at[j], term, sem)
                    copy.start()
                    copy.wait()
                    total[...] += term[...].astype(jnp.float32)

            repeat(requests, add)
            out_ref[s] = total[...].astype(out_ref.dtype)

    repeat(requests, visit)


def home_kernel(chips, where_ref, final_ref, own_ref, other_ref, down_zero_ref, up_zero_ref, down_ref, up_ref, stage, in_sems, out_sems):
    held = down_ref.shape[0]
    part = own_ref.shape[3]
    core = where_ref[1] % 2
    room = stage.shape[0]

    def each(act):
        def visit(a, n):
            slot = final_ref[a]

            @pl.when(slot >= 0)
            def _():
                act(a, slot, n)

            return n + (slot >= 0).astype(jnp.int32)

        lax.fori_loop(0, held, visit, 0)

    def gathers(do):
        def act(a, slot, n):
            for kind in range(2):
                for near, ref in ((True, own_ref), (False, other_ref)):

                    @pl.when((core == kind) == near)
                    def _(kind=kind, ref=ref):
                        for p in range(chips):
                            do(pltpu.make_async_copy(ref.at[p, slot], stage.at[n, kind, :, pl.ds(p * part, part)], in_sems.at[n, kind, p]))

        return act

    def writes(a, n):
        return [pltpu.make_async_copy(stage.at[n, kind], ref.at[a], out_sems.at[n, kind]) for kind, ref in ((0, down_ref), (1, up_ref))]

    def flush(a, slot, n):
        gathers(lambda copy: copy.wait())(a, slot, n)
        for copy in writes(a, n):
            copy.start()

    def finish(a, slot, n):
        for copy in writes(a, n):
            copy.wait()

    each(gathers(lambda copy: copy.start()))
    each(flush)
    each(finish)


def with_capacity(cap, blocks, where, src, slot, first, count, final, activations, out_grad, down_panels, up_panels, far_down, far_up, gates):
    held, rank, width = down_panels.shape
    chips = blocks // 2
    part = width // chips
    bf16 = jnp.bfloat16
    dma = pltpu.SemaphoreType.DMA
    partner = [(i, i ^ 1) for i in range(blocks)]
    same_core = [[2 * i + c for i in range(chips)] for c in range(2)]

    slices = pl.pallas_call(
        functools.partial(compose_kernel, cap, held, chips),
        out_shape=jax.ShapeDtypeStruct((chips, cap, rank, part), bf16),
        in_specs=[SMEM, SMEM, ANY, ANY, ANY, ANY],
        out_specs=VMEM,
        scratch_shapes=[dma((cap, chips))],
        name="compose",
    )(where, src, down_panels, up_panels, far_down, far_up)
    slices = lax.all_to_all(slices, "blk", 0, 0, tiled=True, axis_index_groups=same_core)

    picked = pl.pallas_call(
        functools.partial(pick_kernel, cap),
        out_shape=jax.ShapeDtypeStruct((2 * blocks, rank, part), bf16),
        in_specs=[SMEM, ANY],
        out_specs=VMEM,
        scratch_shapes=[dma((2 * blocks,))],
        name="pick",
    )(slot, slices.reshape(chips * cap, rank, part))
    panels = lax.all_to_all(picked.reshape(blocks, 2, rank, part), "blk", 0, 0, tiled=True)

    terms = pl.pallas_call(
        terms_kernel,
        out_shape=jax.ShapeDtypeStruct((blocks, 2, rank, part), bf16),
        in_specs=[SMEM, VMEM, VMEM, VMEM],
        out_specs=VMEM,
        name="terms",
    )(gates, activations, out_grad, panels)
    terms = lax.all_to_all(terms, "blk", 0, 0, tiled=True)

    sums = pl.pallas_call(
        functools.partial(merge_kernel, cap),
        out_shape=jax.ShapeDtypeStruct((chips * cap, rank, part), bf16),
        in_specs=[SMEM, SMEM, SMEM, ANY],
        out_specs=VMEM,
        scratch_shapes=[pltpu.VMEM((rank, part), jnp.float32), pltpu.VMEM((rank, part), bf16), dma((2 * blocks,)), dma],
        name="merge",
    )(slot, first, count, terms.reshape(2 * blocks, rank, part))
    own = lax.all_to_all(sums.reshape(chips, cap, rank, part), "blk", 0, 0, tiled=True, axis_index_groups=same_core)
    other = lax.ppermute(own, "blk", partner)

    room = min(cap, held)
    shape = jax.ShapeDtypeStruct((held, rank, width), bf16)
    return pl.pallas_call(
        functools.partial(home_kernel, chips),
        out_shape=(shape, shape),
        in_specs=[SMEM, SMEM, ANY, ANY, ANY, ANY],
        out_specs=(ANY, ANY),
        scratch_shapes=[pltpu.VMEM((room, 2, rank, width), bf16), dma((room, 2, chips)), dma((room, 2))],
        input_output_aliases={4: 0, 5: 1},
        name="home",
    )(where, final, own, other, jnp.zeros(shape.shape, bf16), jnp.zeros(shape.shape, bf16))


def shards(groups, blocks, activations, out_grad, down_panels, up_panels, routes, gates):
    held = down_panels.shape[0]
    chips = blocks // 2
    where = jnp.stack([lax.axis_index("groups"), lax.axis_index("blk")]).astype(jnp.int32)
    far_down = lax.ppermute(down_panels, "blk", [(2 * i + 1, 2 * i) for i in range(chips)])
    far_up = lax.ppermute(up_panels, "blk", [(2 * i, 2 * i + 1) for i in range(chips)])
    copies = jnp.broadcast_to(routes.reshape(1, 1, 2), (groups * blocks, 1, 2))
    routes_all = lax.all_to_all(copies, ("groups", "blk"), 0, 0, tiled=True).reshape(-1)
    requests = 2 * blocks
    sizes = (2 * held, 2 * requests, requests, requests, held, 1)
    src, slot, first, count, final, most = pl.pallas_call(
        functools.partial(tables_kernel, groups, blocks, held),
        out_shape=tuple(jax.ShapeDtypeStruct((n,), jnp.int32) for n in sizes),
        in_specs=[SMEM, SMEM],
        out_specs=(SMEM,) * 6,
        scratch_shapes=[pltpu.SMEM((blocks * held,), jnp.int32), pltpu.SMEM((chips,), jnp.int32)],
        name="tables",
    )(where, routes_all)
    caps = [c for c in CAPACITIES if c < 2 * held] + [2 * held]
    branch = sum((most[0] > c).astype(jnp.int32) for c in caps[:-1])
    return lax.switch(
        branch,
        [functools.partial(with_capacity, c, blocks) for c in caps],
        where, src, slot, first, count, final, activations, out_grad, down_panels, up_panels, far_down, far_up, gates,
    )


def solution(mesh):
    in_specs = (
        P(("groups", "blk"), None),
        P(("groups", "blk"), None),
        P("blk", None, None),
        P("blk", None, None),
        P(("groups", "blk"), None),
        P(("groups", "blk"), None),
    )
    out_specs = (P(("groups", "blk"), None, None), P(("groups", "blk"), None, None))
    body = functools.partial(shards, mesh.shape["groups"], mesh.shape["blk"])
    return jax.shard_map(body, mesh=mesh, in_specs=in_specs, out_specs=out_specs, check_vma=False)
```

```python
import functools

import jax
import jax.numpy as jnp
from jax import lax
from jax.experimental import pallas as pl
from jax.experimental.pallas import tpu as pltpu
from jax.sharding import PartitionSpec as P

ANY = pl.BlockSpec(memory_space=pl.ANY)
SMEM = pl.BlockSpec(memory_space=pltpu.SMEM)
VMEM = pl.BlockSpec(memory_space=pltpu.VMEM)
DMA = pltpu.SemaphoreType.DMA
BF16 = jnp.bfloat16
GROUP_CAPACITIES = (6, 7, 8, 9, 10)
POOL_CAPACITIES = (9, 10, 11, 12, 13, 15)


def repeat(n, body):
    def step(i, carry):
        body(i)
        return carry

    lax.fori_loop(0, n, step, 0)


def branch_of(most, caps):
    return sum((most > c).astype(jnp.int32) for c in caps[:-1])


def tables_kernel(shape, pool_caps, caps, where_ref, routes_ref, src_ref, pool_ref, slot_ref, first_ref, final_ref, branch_ref, seen, load):
    groups, blocks, held, pooled = shape
    requests = 2 * blocks
    chips = blocks // 2
    group, me = where_ref[0], where_ref[1]
    chip = lax.div(me, 2)
    zero = jnp.int32(0)

    def clear(ref, n, value):
        def body(i):
            ref[i] = value

        repeat(n, body)

    def scan(base, n, most, write):
        clear(load, chips, 0)

        def unsee(i):
            seen[routes_ref[base + lax.div(i, 2), 0, lax.rem(i, 2)]] = -1

        repeat(n, unsee)

        def visit(i, most):
            adapter = routes_ref[base + lax.div(i, 2), 0, lax.rem(i, 2)]
            before = seen[adapter]
            new = before < 0
            owner = lax.div(adapter, 2 * held)
            filled = load[owner]
            rank = jnp.where(new, filled, before)
            seen[adapter] = rank
            filled = filled + new.astype(jnp.int32)
            load[owner] = filled
            if write is not None:
                write(i, adapter, owner, new, rank)
            return jnp.maximum(most, filled)

        return lax.fori_loop(0, n, visit, most)

    clear(src_ref, 2 * held, -1)
    clear(final_ref, held, -1)

    def write_pool(i, adapter, owner, new, rank):
        pool_ref[2 * i] = owner
        pool_ref[2 * i + 1] = rank
        src_ref[jnp.where(owner == chip, rank, 2 * held)] = adapter - owner * (2 * held)

    def write_group(i, adapter, owner, new, rank):
        slot_ref[2 * i] = owner
        slot_ref[2 * i + 1] = rank
        first_ref[i] = new.astype(jnp.int32)
        final_ref[jnp.where(lax.div(adapter, held) == me, adapter - me * held, held)] = rank

    def others(most):
        return lax.fori_loop(0, groups - 1, lambda g, m: scan(jnp.where(g < group, g, g + 1) * blocks, requests, m, None), most)

    pool_most = scan(zero if pooled else group * blocks, requests * (groups if pooled else 1), zero, write_pool)
    most = others(scan(group * blocks, requests, zero, write_group))
    branch_ref[0] = branch_of(pool_most if pooled else most, pool_caps)
    branch_ref[1] = branch_of(most, caps)


def compose_kernel(cap, held, chips, pooled, where_ref, src_ref, down_ref, up_ref, far_down_ref, far_up_ref, out_ref, sems):
    part = out_ref.shape[3]
    core = lax.rem(where_ref[1], 2)
    base = where_ref[0] * (part * chips) if pooled else 0

    def each(act):
        def visit(c):
            adapter = src_ref[c]
            near = lax.div(adapter, held) == core
            a = lax.rem(adapter, held)
            for kind, sources in ((0, (far_down_ref, down_ref)), (1, (far_up_ref, up_ref))):
                for own in (0, 1):

                    @pl.when((adapter >= 0) & (core == kind) & (near == (own == 1)))
                    def _(ref=sources[own]):
                        def slices(p):
                            cols = pl.ds(pl.multiple_of(base + p * part, 128), part)
                            act(pltpu.make_async_copy(ref.at[a, :, cols], out_ref.at[p, c], sems.at[c, p]))

                        repeat(chips, slices)

        repeat(cap, visit)

    each(lambda copy: copy.start())
    each(lambda copy: copy.wait())


def pick_kernel(cap, pool_ref, held_ref, out_ref):
    def visit(i):
        out_ref[i] = held_ref[pool_ref[2 * i] * cap + pool_ref[2 * i + 1]]

    repeat(out_ref.shape[0], visit)


def terms_kernel(blocks, gates_ref, rows_ref, grads_ref, panels_ref, out_ref):
    devices, slots, rank, part = panels_ref.shape
    tokens = rows_ref.shape[0]
    last = (((1,), (1,)), ((), ()))

    def gather(s, sums):
        low, back = sums
        cols = pl.ds(pl.multiple_of(s * part, 128), part)
        down = panels_ref[2 * s].reshape(slots * rank, part)
        up = panels_ref[2 * s + 1].reshape(slots * rank, part)
        low += lax.dot_general(down, rows_ref[:, cols], last, preferred_element_type=jnp.float32)
        back += lax.dot_general(up, grads_ref[:, cols], last, preferred_element_type=jnp.float32)
        return low, back

    zero = jnp.zeros((slots * rank, tokens), jnp.float32)
    low, back = lax.fori_loop(0, devices // 2, gather, (zero, zero), unroll=2)
    low, back = low.astype(BF16), back.astype(BF16)
    wide = out_ref.shape[3]

    def spread(p, _):
        cols = pl.ds(pl.multiple_of(p * wide, 128), wide)
        down = jnp.dot(back, rows_ref[:, cols], preferred_element_type=jnp.float32)
        up = jnp.dot(low, grads_ref[:, cols], preferred_element_type=jnp.float32)
        for k in range(slots):
            gate = gates_ref[0, k]
            out_ref[2 * p, k] = (down[k * rank : (k + 1) * rank] * gate).astype(out_ref.dtype)
            out_ref[2 * p + 1, k] = (up[k * rank : (k + 1) * rank] * gate).astype(out_ref.dtype)
        return 0

    lax.fori_loop(0, blocks // 2, spread, 0, unroll=2)


def merge_kernel(cap, slot_ref, first_ref, terms_ref, out_ref, total):
    requests = terms_ref.shape[0]

    def slot(i):
        return slot_ref[2 * i] * cap + slot_ref[2 * i + 1]

    def place(i, again):
        @pl.when(first_ref[i] == 1)
        def _():
            out_ref[slot(i)] = terms_ref[i]

        return again + 1 - first_ref[i]

    again = lax.fori_loop(0, requests, place, jnp.int32(0))

    @pl.when(again > 0)
    def _():
        def visit(i):
            s = slot(i)

            @pl.when(first_ref[i] == 1)
            def _():
                total[...] = terms_ref[i].astype(jnp.float32)

                def add(j, n):
                    same = (j > i) & (slot(j) == s)

                    @pl.when(same)
                    def _():
                        total[...] += terms_ref[j].astype(jnp.float32)

                    return n + same.astype(jnp.int32)

                more = lax.fori_loop(0, requests, add, jnp.int32(0))

                @pl.when(more > 0)
                def _():
                    out_ref[s] = total[...].astype(out_ref.dtype)

        repeat(requests, visit)


def zeros_kernel(after_ref, down_ref, up_ref, zero, sems):
    held = down_ref.shape[0]
    zero[...] = jnp.zeros_like(zero)

    def each(act):
        def visit(a):
            act(pltpu.make_async_copy(zero, down_ref.at[a], sems.at[a, 0]))
            act(pltpu.make_async_copy(zero, up_ref.at[a], sems.at[a, 1]))

        repeat(held, visit)

    each(lambda copy: copy.start())
    each(lambda copy: copy.wait())


def home_kernel(chips, where_ref, final_ref, own_ref, other_ref, down_zero_ref, up_zero_ref, down_ref, up_ref, sems):
    held = down_ref.shape[0]
    part = own_ref.shape[3]
    core = lax.rem(where_ref[1], 2)

    def each(act):
        def visit(a):
            slot = final_ref[a]
            for swap in (0, 1):

                @pl.when((slot >= 0) & (core == swap))
                def _():
                    for kind, out in ((0, down_ref), (1, up_ref)):
                        source = own_ref if kind == swap else other_ref

                        def slices(p, source=source, out=out, kind=kind):
                            cols = pl.ds(pl.multiple_of(p * part, 128), part)
                            act(pltpu.make_async_copy(source.at[p, slot], out.at[a, :, cols], sems.at[a, kind, p]))

                        repeat(chips, slices)

        repeat(held, visit)

    each(lambda copy: copy.start())
    each(lambda copy: copy.wait())


def fetch(cap, axes, pooled, blocks, where, src, pool, down_panels, up_panels, far_down, far_up):
    held, rank, width = down_panels.shape
    chips = blocks // 2
    requests = pool.shape[0] // 2
    part = width // (chips * (requests // (2 * blocks)))
    same_core = [[2 * i + c for i in range(chips)] for c in range(2)]
    slices = pl.pallas_call(
        functools.partial(compose_kernel, cap, held, chips, pooled),
        out_shape=jax.ShapeDtypeStruct((chips, cap, rank, part), BF16),
        in_specs=[SMEM, SMEM, ANY, ANY, ANY, ANY],
        out_specs=VMEM,
        scratch_shapes=[DMA((cap, chips))],
        name="compose",
    )(where, src, down_panels, up_panels, far_down, far_up)
    slices = lax.all_to_all(slices, "blk", 0, 0, tiled=True, axis_index_groups=same_core)
    picked = pl.pallas_call(
        functools.partial(pick_kernel, cap),
        out_shape=jax.ShapeDtypeStruct((requests, rank, part), BF16),
        in_specs=[SMEM, VMEM],
        out_specs=VMEM,
        name="pick",
    )(pool, slices.reshape(chips * cap, rank, part))
    return lax.all_to_all(picked.reshape(requests // 2, 2, rank, part), axes, 0, 0, tiled=True)


def give_back(cap, blocks, held, where, slot, first, final, terms):
    _, _, rank, part = terms.shape
    chips = blocks // 2
    width = part * chips
    partner = [(i, i ^ 1) for i in range(blocks)]
    same_core = [[2 * i + c for i in range(chips)] for c in range(2)]
    sums = pl.pallas_call(
        functools.partial(merge_kernel, cap),
        out_shape=jax.ShapeDtypeStruct((chips * cap, rank, part), BF16),
        in_specs=[SMEM, SMEM, VMEM],
        out_specs=VMEM,
        scratch_shapes=[pltpu.VMEM((rank, part), jnp.float32)],
        name="merge",
    )(slot, first, terms.reshape(2 * blocks, rank, part))
    own = lax.all_to_all(sums.reshape(chips, cap, rank, part), "blk", 0, 0, tiled=True, axis_index_groups=same_core)
    shape = jax.ShapeDtypeStruct((held, rank, width), BF16)
    zeros = pl.pallas_call(
        zeros_kernel,
        out_shape=(shape, shape),
        in_specs=[ANY],
        out_specs=(ANY, ANY),
        scratch_shapes=[pltpu.VMEM((rank, width), BF16), DMA((held, 2))],
        cost_estimate=pl.CostEstimate(flops=0, bytes_accessed=4 * held * rank * width, transcendentals=0),
        name="zeros",
    )(sums)
    own, zeros = lax.optimization_barrier((own, zeros))
    other = lax.ppermute(own, "blk", partner)
    return pl.pallas_call(
        functools.partial(home_kernel, chips),
        out_shape=(shape, shape),
        in_specs=[SMEM, SMEM, VMEM, VMEM, ANY, ANY],
        out_specs=(ANY, ANY),
        scratch_shapes=[DMA((held, 2, chips))],
        input_output_aliases={4: 0, 5: 1},
        name="home",
    )(where, final, own, other, *zeros)


def shards(groups, blocks, activations, out_grad, down_panels, up_panels, routes, gates):
    held, rank, width = down_panels.shape
    chips = blocks // 2
    requests = 2 * blocks
    pooled = groups > 1 and width % (128 * chips * groups) == 0
    caps = [c for c in GROUP_CAPACITIES if c < 2 * held] + [2 * held]
    pool_caps = [c for c in POOL_CAPACITIES if c < 2 * held] + [2 * held] if pooled else caps

    where = jnp.stack([lax.axis_index("groups"), lax.axis_index("blk")]).astype(jnp.int32)
    far_down = lax.ppermute(down_panels, "blk", [(2 * i + 1, 2 * i) for i in range(chips)])
    far_up = lax.ppermute(up_panels, "blk", [(2 * i, 2 * i + 1) for i in range(chips)])
    copies = jnp.broadcast_to(routes.reshape(1, 1, 2), (groups * blocks, 1, 2))
    routes_all = lax.all_to_all(copies, ("groups", "blk"), 0, 0, tiled=True)
    sizes = (2 * held + 1, 2 * requests * (groups if pooled else 1), 2 * requests, requests, held + 1, 2)
    src, pool, slot, first, final, branch = pl.pallas_call(
        functools.partial(tables_kernel, (groups, blocks, held, pooled), pool_caps, caps),
        out_shape=tuple(jax.ShapeDtypeStruct((n,), jnp.int32) for n in sizes),
        in_specs=[SMEM, SMEM],
        out_specs=(SMEM,) * len(sizes),
        scratch_shapes=[pltpu.SMEM((blocks * held,), jnp.int32), pltpu.SMEM((chips,), jnp.int32)],
        name="tables",
    )(where, routes_all)

    panels = lax.switch(
        branch[0],
        [functools.partial(fetch, c, ("groups", "blk") if pooled else "blk", pooled, blocks) for c in pool_caps],
        where, src, pool, down_panels, up_panels, far_down, far_up,
    )
    terms = pl.pallas_call(
        functools.partial(terms_kernel, blocks),
        out_shape=jax.ShapeDtypeStruct((blocks, 2, rank, width // chips), BF16),
        in_specs=[SMEM, VMEM, VMEM, VMEM],
        out_specs=VMEM,
        name="terms",
    )(gates, activations, out_grad, panels)
    terms = lax.all_to_all(terms, "blk", 0, 0, tiled=True)
    return lax.switch(
        branch[1],
        [functools.partial(give_back, c, blocks, held) for c in caps],
        where, slot, first, final, terms,
    )


def solution(mesh):
    in_specs = (
        P(("groups", "blk"), None),
        P(("groups", "blk"), None),
        P("blk", None, None),
        P("blk", None, None),
        P(("groups", "blk"), None),
        P(("groups", "blk"), None),
    )
    out_specs = (P(("groups", "blk"), None, None), P(("groups", "blk"), None, None))
    body = functools.partial(shards, mesh.shape["groups"], mesh.shape["blk"])
    return jax.shard_map(body, mesh=mesh, in_specs=in_specs, out_specs=out_specs, check_vma=False)
```

```python
import functools

import jax
import jax.numpy as jnp
from jax import lax
from jax.experimental import pallas as pl
from jax.experimental.pallas import tpu as pltpu
from jax.sharding import PartitionSpec as P

ANY = pl.BlockSpec(memory_space=pl.ANY)
HBM = pl.BlockSpec(memory_space=pltpu.HBM)
SMEM = pl.BlockSpec(memory_space=pltpu.SMEM)
VMEM = pl.BlockSpec(memory_space=pltpu.VMEM)
DMA = pltpu.SemaphoreType.DMA
BF16 = jnp.bfloat16
GROUP_CAPACITIES = (6, 7, 8, 9, 10)
POOL_CAPACITIES = (9, 10, 11, 12, 13, 15)


def repeat(n, body):
    def step(i, carry):
        body(i)
        return carry

    lax.fori_loop(0, n, step, 0)


def branch_of(most, caps):
    return sum((most > c).astype(jnp.int32) for c in caps[:-1])


def tables_kernel(shape, pool_caps, caps, where_ref, routes_ref, src_ref, pool_ref, slot_ref, count_ref, final_ref, branch_ref, pool_seen, pool_load, seen, load, origin):
    groups, blocks, held, pooled = shape
    requests = 2 * blocks
    chips = blocks // 2
    group, me = where_ref[0], where_ref[1]
    chip = lax.div(me, 2)
    zero = jnp.int32(0)

    def clear(ref, n, value):
        def body(i):
            ref[i] = value

        repeat(n, body)

    def rank_of(seen, load, adapter, owner):
        before = seen[adapter]
        new = before < 0
        filled = load[owner]
        rank = jnp.where(new, filled, before)
        seen[adapter] = rank
        filled = filled + new.astype(jnp.int32)
        load[owner] = filled
        return rank, new, filled

    clear(src_ref, 2 * held, -1)
    clear(final_ref, held, -1)
    clear(pool_load, chips, 0)

    def scan(g, most, mine):
        clear(load, chips, 0)

        def unsee(b):
            for k in range(2):
                adapter = routes_ref[g * blocks + b, 0, k]
                seen[adapter] = -1

        repeat(blocks, unsee)

        def visit(b, most):
            most, pool_most = most
            for k in range(2):
                i = 2 * b + k
                adapter = routes_ref[g * blocks + b, 0, k]
                owner = lax.div(adapter, 2 * held)
                rank, new, filled = rank_of(seen, load, adapter, owner)
                most = jnp.maximum(most, filled)
                if pooled:
                    pool_rank, _, filled = rank_of(pool_seen, pool_load, adapter, owner)
                    pool_most = jnp.maximum(pool_most, filled)
                    at = 2 * (g * requests + i)
                else:
                    pool_rank, at = rank, 2 * i
                if pooled or mine:
                    pool_ref[at] = owner
                    pool_ref[at + 1] = pool_rank
                    src_ref[jnp.where(owner == chip, pool_rank, 2 * held)] = adapter - owner * (2 * held)
                if mine:
                    slot_ref[2 * i] = owner
                    slot_ref[2 * i + 1] = rank
                    count_ref[i] = 0
                    start = jnp.where(new, i, origin[adapter])
                    origin[adapter] = start
                    count_ref[start] = count_ref[start] + 1
                    final_ref[jnp.where(lax.div(adapter, held) == me, adapter - me * held, held)] = rank
            return most, pool_most

        return lax.fori_loop(0, blocks, visit, most)

    if pooled:

        def unsee(b):
            for k in range(2):
                pool_seen[routes_ref[b, 0, k]] = -1

        repeat(groups * blocks, unsee)
    most = scan(group, (zero, zero), True)
    most, pool_most = lax.fori_loop(0, groups - 1, lambda g, m: scan(jnp.where(g < group, g, g + 1), m, False), most)
    branch_ref[0] = branch_of(pool_most if pooled else most, pool_caps)
    branch_ref[1] = branch_of(most, caps)


def compose_kernel(cap, held, chips, pooled, where_ref, src_ref, down_ref, up_ref, far_down_ref, far_up_ref, out_ref, sems):
    part = out_ref.shape[3]
    core = lax.rem(where_ref[1], 2)
    base = where_ref[0] * (part * chips) if pooled else 0

    def each(act):
        def visit(c):
            adapter = src_ref[c]
            near = lax.div(adapter, held) == core
            a = lax.rem(adapter, held)
            for kind, sources in ((0, (far_down_ref, down_ref)), (1, (far_up_ref, up_ref))):
                for own in (0, 1):

                    @pl.when((adapter >= 0) & (core == kind) & (near == (own == 1)))
                    def _(ref=sources[own]):
                        def slices(p):
                            cols = pl.ds(pl.multiple_of(base + p * part, 128), part)
                            act(pltpu.make_async_copy(ref.at[a, :, cols], out_ref.at[p, c], sems.at[c, p]))

                        repeat(chips, slices)

        repeat(cap, visit)

    each(lambda copy: copy.start())
    each(lambda copy: copy.wait())


def pick_kernel(cap, pool_ref, held_ref, out_ref):
    def visit(i):
        out_ref[i] = held_ref[pool_ref[2 * i] * cap + pool_ref[2 * i + 1]]

    repeat(out_ref.shape[0], visit)


def terms_kernel(blocks, gates_ref, rows_ref, grads_ref, panels_ref, out_ref):
    devices, slots, rank, part = panels_ref.shape
    tokens = rows_ref.shape[0]
    last = (((1,), (1,)), ((), ()))

    def gather(s, sums):
        low, back = sums
        cols = pl.ds(pl.multiple_of(s * part, 128), part)
        down = panels_ref[2 * s].reshape(slots * rank, part)
        up = panels_ref[2 * s + 1].reshape(slots * rank, part)
        low += lax.dot_general(down, rows_ref[:, cols], last, preferred_element_type=jnp.float32)
        back += lax.dot_general(up, grads_ref[:, cols], last, preferred_element_type=jnp.float32)
        return low, back

    zero = jnp.zeros((slots * rank, tokens), jnp.float32)
    low, back = lax.fori_loop(0, devices // 2, gather, (zero, zero), unroll=2)
    low, back = low.astype(BF16), back.astype(BF16)
    wide = out_ref.shape[3]

    def spread(p, _):
        cols = pl.ds(pl.multiple_of(p * wide, 128), wide)
        down = jnp.dot(back, rows_ref[:, cols], preferred_element_type=jnp.float32)
        up = jnp.dot(low, grads_ref[:, cols], preferred_element_type=jnp.float32)
        for k in range(slots):
            gate = gates_ref[0, k]
            out_ref[2 * p, k] = (down[k * rank : (k + 1) * rank] * gate).astype(out_ref.dtype)
            out_ref[2 * p + 1, k] = (up[k * rank : (k + 1) * rank] * gate).astype(out_ref.dtype)
        return 0

    lax.fori_loop(0, blocks // 2, spread, 0, unroll=2)


def merge_kernel(cap, slot_ref, count_ref, terms_ref, out_ref, total):
    requests = terms_ref.shape[0]

    def slot(i):
        return slot_ref[2 * i] * cap + slot_ref[2 * i + 1]

    def visit(i):
        @pl.when(count_ref[i] == 1)
        def _():
            out_ref[slot(i)] = terms_ref[i]

        @pl.when(count_ref[i] > 1)
        def _():
            s = slot(i)
            total[...] = terms_ref[i].astype(jnp.float32)

            def add(j, _):
                @pl.when(slot(j) == s)
                def _():
                    total[...] += terms_ref[j].astype(jnp.float32)

                return 0

            lax.fori_loop(i + 1, requests, add, 0)
            out_ref[s] = total[...].astype(out_ref.dtype)

    repeat(requests, visit)


def zeros_kernel(after_ref, down_ref, up_ref, zero, sems):
    held = down_ref.shape[0]
    zero[...] = jnp.zeros_like(zero)

    def each(act):
        def visit(a):
            act(pltpu.make_async_copy(zero, down_ref.at[a], sems.at[a, 0]))
            act(pltpu.make_async_copy(zero, up_ref.at[a], sems.at[a, 1]))

        repeat(held, visit)

    each(lambda copy: copy.start())
    each(lambda copy: copy.wait())


def home_kernel(chips, where_ref, final_ref, own_ref, other_ref, down_zero_ref, up_zero_ref, down_ref, up_ref, stage, in_sems, out_sems):
    held = down_ref.shape[0]
    part = own_ref.shape[3]
    core = lax.rem(where_ref[1], 2)

    def each(act):
        def visit(a, n):
            slot = final_ref[a]

            @pl.when(slot >= 0)
            def _():
                act(a, slot, n)

            return n + (slot >= 0).astype(jnp.int32)

        lax.fori_loop(0, held, visit, jnp.int32(0))

    def gathers(do):
        def act(a, slot, n):
            for swap in (0, 1):

                @pl.when(core == swap)
                def _(swap=swap):
                    for kind in range(2):
                        source = own_ref if kind == swap else other_ref
                        for p in range(chips):
                            do(pltpu.make_async_copy(source.at[p, slot], stage.at[n, kind, :, pl.ds(p * part, part)], in_sems.at[n, kind, p]))

        return act

    def writes(a, n):
        return [pltpu.make_async_copy(stage.at[n, kind], ref.at[a], out_sems.at[n, kind]) for kind, ref in ((0, down_ref), (1, up_ref))]

    def flush(a, slot, n):
        gathers(lambda copy: copy.wait())(a, slot, n)
        for copy in writes(a, n):
            copy.start()

    def finish(a, slot, n):
        for copy in writes(a, n):
            copy.wait()

    each(gathers(lambda copy: copy.start()))
    each(flush)
    each(finish)


def fetch(cap, axes, pooled, blocks, where, src, pool, down_panels, up_panels, far_down, far_up):
    held, rank, width = down_panels.shape
    chips = blocks // 2
    requests = pool.shape[0] // 2
    part = width // (chips * (requests // (2 * blocks)))
    same_core = [[2 * i + c for i in range(chips)] for c in range(2)]
    slices = pl.pallas_call(
        functools.partial(compose_kernel, cap, held, chips, pooled),
        out_shape=jax.ShapeDtypeStruct((chips, cap, rank, part), BF16),
        in_specs=[SMEM, SMEM, ANY, ANY, ANY, ANY],
        out_specs=VMEM,
        scratch_shapes=[DMA((cap, chips))],
        name="compose",
    )(where, src, down_panels, up_panels, far_down, far_up)
    slices = lax.all_to_all(slices, "blk", 0, 0, tiled=True, axis_index_groups=same_core)
    picked = pl.pallas_call(
        functools.partial(pick_kernel, cap),
        out_shape=jax.ShapeDtypeStruct((requests, rank, part), BF16),
        in_specs=[SMEM, VMEM],
        out_specs=VMEM,
        name="pick",
    )(pool, slices.reshape(chips * cap, rank, part))
    return lax.all_to_all(picked.reshape(requests // 2, 2, rank, part), axes, 0, 0, tiled=True)


def give_back(cap, blocks, held, where, slot, count, final, terms):
    _, _, rank, part = terms.shape
    chips = blocks // 2
    width = part * chips
    partner = [(i, i ^ 1) for i in range(blocks)]
    same_core = [[2 * i + c for i in range(chips)] for c in range(2)]
    sums = pl.pallas_call(
        functools.partial(merge_kernel, cap),
        out_shape=jax.ShapeDtypeStruct((chips * cap, rank, part), BF16),
        in_specs=[SMEM, SMEM, VMEM],
        out_specs=VMEM,
        scratch_shapes=[pltpu.VMEM((rank, part), jnp.float32)],
        name="merge",
    )(slot, count, terms.reshape(2 * blocks, rank, part))
    own = lax.all_to_all(sums.reshape(chips, cap, rank, part), "blk", 0, 0, tiled=True, axis_index_groups=same_core)
    shape = jax.ShapeDtypeStruct((held, rank, width), BF16)
    zeros = pl.pallas_call(
        zeros_kernel,
        out_shape=(shape, shape),
        in_specs=[ANY],
        out_specs=(ANY, ANY),
        scratch_shapes=[pltpu.VMEM((rank, width), BF16), DMA((held, 2))],
        cost_estimate=pl.CostEstimate(flops=0, bytes_accessed=4 * held * rank * width, transcendentals=0),
        name="zeros",
    )(sums)
    own, zeros = lax.optimization_barrier((own, zeros))
    other = lax.ppermute(own, "blk", partner)
    room = min(cap, held)
    return pl.pallas_call(
        functools.partial(home_kernel, chips),
        out_shape=(shape, shape),
        in_specs=[SMEM, SMEM, HBM, HBM, ANY, ANY],
        out_specs=(ANY, ANY),
        scratch_shapes=[pltpu.VMEM((room, 2, rank, width), BF16), DMA((room, 2, chips)), DMA((room, 2))],
        input_output_aliases={4: 0, 5: 1},
        name="home",
    )(where, final, own, other, *zeros)


def shards(groups, blocks, activations, out_grad, down_panels, up_panels, routes, gates):
    held, rank, width = down_panels.shape
    chips = blocks // 2
    requests = 2 * blocks
    pooled = groups > 1 and width % (128 * chips * groups) == 0
    caps = [c for c in GROUP_CAPACITIES if c < 2 * held] + [2 * held]
    pool_caps = [c for c in POOL_CAPACITIES if c < 2 * held] + [2 * held] if pooled else caps

    where = jnp.stack([lax.axis_index("groups"), lax.axis_index("blk")]).astype(jnp.int32)
    copies = jnp.broadcast_to(routes.reshape(1, 1, 2), (groups * blocks, 1, 2))
    routes_all = lax.all_to_all(copies, ("groups", "blk"), 0, 0, tiled=True)
    near_down, near_up, _ = lax.optimization_barrier((down_panels, up_panels, copies))
    far_down = lax.ppermute(near_down, "blk", [(2 * i + 1, 2 * i) for i in range(chips)])
    far_up = lax.ppermute(near_up, "blk", [(2 * i, 2 * i + 1) for i in range(chips)])
    sizes = (2 * held + 1, 2 * requests * (groups if pooled else 1), 2 * requests, requests, held + 1, 2)
    src, pool, slot, count, final, branch = pl.pallas_call(
        functools.partial(tables_kernel, (groups, blocks, held, pooled), pool_caps, caps),
        out_shape=tuple(jax.ShapeDtypeStruct((n,), jnp.int32) for n in sizes),
        in_specs=[SMEM, SMEM],
        out_specs=(SMEM,) * len(sizes),
        scratch_shapes=[pltpu.SMEM((n,), jnp.int32) for n in (blocks * held, chips, blocks * held, chips, blocks * held)],
        name="tables",
    )(where, routes_all)

    panels = lax.switch(
        branch[0],
        [functools.partial(fetch, c, ("groups", "blk") if pooled else "blk", pooled, blocks) for c in pool_caps],
        where, src, pool, down_panels, up_panels, far_down, far_up,
    )
    terms = pl.pallas_call(
        functools.partial(terms_kernel, blocks),
        out_shape=jax.ShapeDtypeStruct((blocks, 2, rank, width // chips), BF16),
        in_specs=[SMEM, VMEM, VMEM, VMEM],
        out_specs=VMEM,
        name="terms",
    )(gates, activations, out_grad, panels)
    terms = lax.all_to_all(terms, "blk", 0, 0, tiled=True)
    return lax.switch(
        branch[1],
        [functools.partial(give_back, c, blocks, held) for c in caps],
        where, slot, count, final, terms,
    )


def solution(mesh):
    in_specs = (
        P(("groups", "blk"), None),
        P(("groups", "blk"), None),
        P("blk", None, None),
        P("blk", None, None),
        P(("groups", "blk"), None),
        P(("groups", "blk"), None),
    )
    out_specs = (P(("groups", "blk"), None, None), P(("groups", "blk"), None, None))
    body = functools.partial(shards, mesh.shape["groups"], mesh.shape["blk"])
    return jax.shard_map(body, mesh=mesh, in_specs=in_specs, out_specs=out_specs, check_vma=False)
```

```python
import functools

import jax
import jax.numpy as jnp
from jax import lax
from jax.experimental import pallas as pl
from jax.experimental.pallas import tpu as pltpu
from jax.sharding import PartitionSpec as P

ANY = pl.BlockSpec(memory_space=pl.ANY)
HBM = pl.BlockSpec(memory_space=pltpu.HBM)
SMEM = pl.BlockSpec(memory_space=pltpu.SMEM)
VMEM = pl.BlockSpec(memory_space=pltpu.VMEM)
DMA = pltpu.SemaphoreType.DMA
BF16 = jnp.bfloat16
GROUP_CAPACITIES = (6, 7, 8, 9, 10)
POOL_CAPACITIES = (9, 10, 11, 12, 13, 15)


def room_for(elements):
    return pltpu.CompilerParams(vmem_limit_bytes=2 * elements + (3 << 20))


def repeat(n, body):
    def step(i, carry):
        body(i)
        return carry

    lax.fori_loop(0, n, step, 0)


def branch_of(most, caps):
    return sum((most > c).astype(jnp.int32) for c in caps[:-1])


def tables_kernel(shape, pool_caps, caps, where_ref, routes_ref, src_ref, pool_ref, slot_ref, count_ref, final_ref, pool_branch_ref, branch_ref, pool_seen, pool_load, seen, load, origin):
    groups, blocks, held, pooled = shape
    requests = 2 * blocks
    chips = blocks // 2
    group, me = where_ref[0], where_ref[1]
    chip = lax.div(me, 2)
    zero = jnp.int32(0)

    def clear(ref, n, value):
        def body(i):
            ref[i] = value

        repeat(n, body)

    def rank_of(seen, load, adapter, owner):
        before = seen[adapter]
        new = before < 0
        filled = load[owner]
        rank = jnp.where(new, filled, before)
        seen[adapter] = rank
        filled = filled + new.astype(jnp.int32)
        load[owner] = filled
        return rank, new, filled

    clear(src_ref, 2 * held, -1)
    clear(final_ref, held, -1)
    clear(pool_load, chips, 0)

    def scan(g, most, mine):
        clear(load, chips, 0)

        def unsee(b):
            for k in range(2):
                adapter = routes_ref[g * blocks + b, 0, k]
                seen[adapter] = -1

        repeat(blocks, unsee)

        def visit(b, most):
            most, pool_most = most
            for k in range(2):
                i = 2 * b + k
                adapter = routes_ref[g * blocks + b, 0, k]
                owner = lax.div(adapter, 2 * held)
                rank, new, filled = rank_of(seen, load, adapter, owner)
                most = jnp.maximum(most, filled)
                if pooled:
                    pool_rank, _, filled = rank_of(pool_seen, pool_load, adapter, owner)
                    pool_most = jnp.maximum(pool_most, filled)
                    at = 2 * (g * requests + i)
                else:
                    pool_rank, at = rank, 2 * i
                if pooled or mine:
                    pool_ref[at] = owner
                    pool_ref[at + 1] = pool_rank
                    src_ref[jnp.where(owner == chip, pool_rank, 2 * held)] = adapter - owner * (2 * held)
                if mine:
                    slot_ref[2 * i] = owner
                    slot_ref[2 * i + 1] = rank
                    count_ref[i] = 0
                    start = jnp.where(new, i, origin[adapter])
                    origin[adapter] = start
                    count_ref[start] = count_ref[start] + 1
                    final_ref[jnp.where(lax.div(adapter, held) == me, adapter - me * held, held)] = rank
            return most, pool_most

        return lax.fori_loop(0, blocks, visit, most)

    if pooled:

        def unsee(b):
            for k in range(2):
                pool_seen[routes_ref[b, 0, k]] = -1

        repeat(groups * blocks, unsee)
    most = scan(group, (zero, zero), True)
    most, pool_most = lax.fori_loop(0, groups - 1, lambda g, m: scan(jnp.where(g < group, g, g + 1), m, False), most)
    pool_branch_ref[0] = branch_of(pool_most if pooled else most, pool_caps)
    branch_ref[0] = branch_of(most, caps)


def take_slots(held, core, src_ref, cap, near, act):
    def visit(c):
        adapter = src_ref[c]

        @pl.when((adapter >= 0) & ((lax.div(adapter, held) == core) == near))
        def _():
            act(c, lax.rem(adapter, held))

    repeat(cap, visit)


def load_slots(cap, held, kind, core, columns, src_ref, panels, to_ref, sems):
    def each(do):
        for k in range(2):

            @pl.when(kind == k)
            def _(k=k):
                def act(c, a):
                    do(c, pltpu.make_async_copy(panels[k].at[a, :, columns], to_ref.at[c], sems.at[c]))

                take_slots(held, core, src_ref, cap, True, act)

    return each


def hand_over_kernel(cap, held, pooled, where_ref, src_ref, down_ref, up_ref, out_ref, sems):
    wide = out_ref.shape[2]
    core = lax.rem(where_ref[1], 2)
    columns = pl.ds(pl.multiple_of(where_ref[0] * wide, 128) if pooled else 0, wide)
    each = load_slots(cap, held, 1 - core, core, columns, src_ref, (down_ref, up_ref), out_ref, sems)
    each(lambda c, copy: copy.start())
    each(lambda c, copy: copy.wait())


def cut(chips, part, from_ref, out_ref, sems, act):
    def slot(c):
        def slices(p):
            act(pltpu.make_async_copy(from_ref.at[c, :, pl.ds(pl.multiple_of(p * part, 128), part)], out_ref.at[p, c], sems.at[c, p]))

        repeat(chips, slices)

    return slot


def near_kernel(cap, held, chips, pooled, where_ref, src_ref, down_ref, up_ref, out_ref, stage, sems, out_sems):
    part = out_ref.shape[3]
    wide = stage.shape[2]
    core = lax.rem(where_ref[1], 2)
    columns = pl.ds(pl.multiple_of(where_ref[0] * wide, 128) if pooled else 0, wide)
    each = load_slots(cap, held, core, core, columns, src_ref, (down_ref, up_ref), stage, sems)
    start = cut(chips, part, stage, out_ref, out_sems, lambda copy: copy.start())
    wait = cut(chips, part, stage, out_ref, out_sems, lambda copy: copy.wait())

    def flush(c, copy):
        copy.wait()
        start(c)

    each(lambda c, copy: copy.start())
    each(flush)
    take_slots(held, core, src_ref, cap, True, lambda c, a: wait(c))


def far_kernel(cap, held, chips, where_ref, src_ref, other_ref, near_ref, out_ref, sems):
    part = out_ref.shape[3]
    core = lax.rem(where_ref[1], 2)
    start = cut(chips, part, other_ref, out_ref, sems, lambda copy: copy.start())
    wait = cut(chips, part, other_ref, out_ref, sems, lambda copy: copy.wait())
    take_slots(held, core, src_ref, cap, False, lambda c, a: start(c))
    take_slots(held, core, src_ref, cap, False, lambda c, a: wait(c))


def pick_kernel(cap, pool_ref, held_ref, out_ref):
    def visit(i):
        out_ref[i] = held_ref[pool_ref[2 * i] * cap + pool_ref[2 * i + 1]]

    repeat(out_ref.shape[0], visit)


def terms_kernel(blocks, gates_ref, rows_ref, grads_ref, panels_ref, out_ref, rows, grads, stage, in_sems, out_sems):
    devices, slots, rank, part = panels_ref.shape
    tokens = rows_ref.shape[0]
    last = (((1,), (1,)), ((), ()))

    def loads(s):
        cols = pl.ds(pl.multiple_of(s * part, 128), part)
        return (
            pltpu.make_async_copy(rows_ref.at[:, cols], rows.at[:, cols], in_sems.at[s, 0]),
            pltpu.make_async_copy(grads_ref.at[:, cols], grads.at[:, cols], in_sems.at[s, 1]),
        )

    def load(s):
        for copy in loads(s):
            copy.start()

    repeat(devices // 2, load)

    def gather(s, sums):
        low, back = sums
        for copy in loads(s):
            copy.wait()
        cols = pl.ds(pl.multiple_of(s * part, 128), part)
        down = panels_ref[2 * s].reshape(slots * rank, part)
        up = panels_ref[2 * s + 1].reshape(slots * rank, part)
        low += lax.dot_general(down, rows[:, cols], last, preferred_element_type=jnp.float32)
        back += lax.dot_general(up, grads[:, cols], last, preferred_element_type=jnp.float32)
        return low, back

    zero = jnp.zeros((slots * rank, tokens), jnp.float32)
    low, back = lax.fori_loop(0, devices // 2, gather, (zero, zero), unroll=4)
    low, back = low.astype(BF16), back.astype(BF16)
    wide = out_ref.shape[3]

    def write(p):
        return pltpu.make_async_copy(stage.at[pl.ds(2 * p, 2)], out_ref.at[pl.ds(2 * p, 2)], out_sems.at[p])

    def spread(p):
        cols = pl.ds(pl.multiple_of(p * wide, 128), wide)
        down = jnp.dot(back, rows[:, cols], preferred_element_type=jnp.float32)
        up = jnp.dot(low, grads[:, cols], preferred_element_type=jnp.float32)
        for k in range(slots):
            gate = gates_ref[0, k]
            stage[2 * p, k] = (down[k * rank : (k + 1) * rank] * gate).astype(out_ref.dtype)
            stage[2 * p + 1, k] = (up[k * rank : (k + 1) * rank] * gate).astype(out_ref.dtype)
        write(p).start()

    repeat(blocks // 2, spread)
    repeat(blocks // 2, lambda p: write(p).wait())


def merge_kernel(cap, slot_ref, count_ref, terms_ref, out_ref, done_ref, total, rounded, sems, sem):
    requests = terms_ref.shape[0]

    def slot(i):
        return slot_ref[2 * i] * cap + slot_ref[2 * i + 1]

    def each(act):
        def visit(i):
            @pl.when(count_ref[i] == 1)
            def _():
                act(pltpu.make_async_copy(terms_ref.at[i], out_ref.at[slot(i)], sems.at[i]))

        repeat(requests, visit)

    each(lambda copy: copy.start())

    def visit(i):
        @pl.when(count_ref[i] > 1)
        def _():
            s = slot(i)
            total[...] = terms_ref[i].astype(jnp.float32)

            def add(j, _):
                @pl.when(slot(j) == s)
                def _():
                    total[...] += terms_ref[j].astype(jnp.float32)

                return 0

            lax.fori_loop(i + 1, requests, add, 0)
            rounded[...] = total[...].astype(rounded.dtype)
            copy = pltpu.make_async_copy(rounded, out_ref.at[s], sem)
            copy.start()
            copy.wait()

    repeat(requests, visit)
    each(lambda copy: copy.wait())
    done_ref[0] = 1


def zeros_kernel(after_ref, down_ref, up_ref, zero, sems):
    held = down_ref.shape[0]
    zero[...] = jnp.zeros_like(zero)

    def each(act):
        def visit(a):
            act(pltpu.make_async_copy(zero, down_ref.at[a], sems.at[a, 0]))
            act(pltpu.make_async_copy(zero, up_ref.at[a], sems.at[a, 1]))

        repeat(held, visit)

    each(lambda copy: copy.start())
    each(lambda copy: copy.wait())


def home_kernel(chips, own, where_ref, final_ref, slices_ref, down_in_ref, up_in_ref, down_ref, up_ref, stage, in_sems, out_sems):
    held = down_ref.shape[0]
    part = slices_ref.shape[3]
    core = lax.rem(where_ref[1], 2)
    kind = core if own else 1 - core

    def each(act):
        def visit(a, n):
            slot = final_ref[a]

            @pl.when(slot >= 0)
            def _():
                act(a, slot, n)

            return n + (slot >= 0).astype(jnp.int32)

        lax.fori_loop(0, held, visit, jnp.int32(0))

    def gather(do):
        def act(a, slot, n):
            for p in range(chips):
                do(pltpu.make_async_copy(slices_ref.at[p, slot], stage.at[n, :, pl.ds(p * part, part)], in_sems.at[n, p]))

        return act

    def write(do):
        def act(a, slot, n):
            for k, ref in ((0, down_ref), (1, up_ref)):

                @pl.when(kind == k)
                def _(ref=ref):
                    do(pltpu.make_async_copy(stage.at[n], ref.at[a], out_sems.at[n]))

        return act

    def flush(a, slot, n):
        gather(lambda copy: copy.wait())(a, slot, n)
        write(lambda copy: copy.start())(a, slot, n)

    each(gather(lambda copy: copy.start()))
    each(flush)
    each(write(lambda copy: copy.wait()))


def fetch(cap, axes, pooled, blocks, where, src, pool, down_panels, up_panels):
    held, rank, width = down_panels.shape
    chips = blocks // 2
    requests = pool.shape[0] // 2
    part = width // (chips * (requests // (2 * blocks)))
    same_core = [[2 * i + c for i in range(chips)] for c in range(2)]
    wide = part * chips
    send = pl.pallas_call(
        functools.partial(hand_over_kernel, cap, held, pooled),
        out_shape=jax.ShapeDtypeStruct((cap, rank, wide), BF16),
        in_specs=[SMEM, SMEM, HBM, HBM],
        out_specs=VMEM,
        scratch_shapes=[DMA((cap,))],
        compiler_params=room_for(cap * rank * wide),
        name="hand_over",
    )(where, src, down_panels, up_panels)
    other = lax.ppermute(send, "blk", [(i, i ^ 1) for i in range(blocks)])
    sliced = jax.ShapeDtypeStruct((chips, cap, rank, part), BF16)
    near = pl.pallas_call(
        functools.partial(near_kernel, cap, held, chips, pooled),
        out_shape=sliced,
        in_specs=[SMEM, SMEM, HBM, HBM],
        out_specs=ANY,
        scratch_shapes=[pltpu.VMEM((cap, rank, wide), BF16), DMA((cap,)), DMA((cap, chips))],
        cost_estimate=pl.CostEstimate(flops=0, bytes_accessed=4 * cap * rank * wide, transcendentals=0),
        compiler_params=pltpu.CompilerParams(vmem_limit_bytes=55 << 20),
        name="near",
    )(where, src, down_panels, up_panels)
    slices = pl.pallas_call(
        functools.partial(far_kernel, cap, held, chips),
        out_shape=sliced,
        in_specs=[SMEM, SMEM, VMEM, ANY],
        out_specs=ANY,
        scratch_shapes=[DMA((cap, chips))],
        input_output_aliases={3: 0},
        compiler_params=room_for(cap * rank * wide),
        name="far",
    )(where, src, other, near)
    slices = lax.all_to_all(slices, "blk", 0, 0, tiled=True, axis_index_groups=same_core)
    picked = pl.pallas_call(
        functools.partial(pick_kernel, cap),
        out_shape=jax.ShapeDtypeStruct((requests, rank, part), BF16),
        in_specs=[SMEM, VMEM],
        out_specs=VMEM,
        compiler_params=room_for((chips * cap + requests) * rank * part),
        name="pick",
    )(pool, slices.reshape(chips * cap, rank, part))
    return lax.all_to_all(picked.reshape(requests // 2, 2, rank, part), axes, 0, 0, tiled=True)


def give_back(cap, blocks, held, where, slot, count, final, terms):
    _, _, rank, part = terms.shape
    chips = blocks // 2
    width = part * chips
    partner = [(i, i ^ 1) for i in range(blocks)]
    same_core = [[2 * i + c for i in range(chips)] for c in range(2)]
    sums, done = pl.pallas_call(
        functools.partial(merge_kernel, cap),
        out_shape=(jax.ShapeDtypeStruct((chips * cap, rank, part), BF16), jax.ShapeDtypeStruct((1,), jnp.int32)),
        in_specs=[SMEM, SMEM, VMEM],
        out_specs=(HBM, SMEM),
        scratch_shapes=[pltpu.VMEM((rank, part), jnp.float32), pltpu.VMEM((rank, part), BF16), DMA((2 * blocks,)), DMA],
        name="merge",
    )(slot, count, terms.reshape(2 * blocks, rank, part))
    own = lax.all_to_all(sums.reshape(chips, cap, rank, part), "blk", 0, 0, tiled=True, axis_index_groups=same_core)
    shape = jax.ShapeDtypeStruct((held, rank, width), BF16)
    zeros = pl.pallas_call(
        zeros_kernel,
        out_shape=(shape, shape),
        in_specs=[SMEM],
        out_specs=(ANY, ANY),
        scratch_shapes=[pltpu.VMEM((rank, width), BF16), DMA((held, 2))],
        cost_estimate=pl.CostEstimate(flops=0, bytes_accessed=4 * held * rank * width, transcendentals=0),
        name="zeros",
    )(done)
    own, grads = lax.optimization_barrier((own, zeros))
    other = lax.ppermute(own, "blk", partner)
    room = min(cap, held)
    for mine, slices in ((True, own), (False, other)):
        grads = pl.pallas_call(
            functools.partial(home_kernel, chips, mine),
            out_shape=(shape, shape),
            in_specs=[SMEM, SMEM, HBM, ANY, ANY],
            out_specs=(ANY, ANY),
            scratch_shapes=[pltpu.VMEM((room, rank, width), BF16), DMA((room, chips)), DMA((room,))],
            input_output_aliases={3: 0, 4: 1},
            cost_estimate=pl.CostEstimate(flops=0, bytes_accessed=4 * room * rank * width, transcendentals=0),
            compiler_params=room_for(room * rank * width),
            name="home_own" if mine else "home_other",
        )(where, final, slices, *grads)
    return grads


def shards(groups, blocks, activations, out_grad, down_panels, up_panels, routes, gates):
    held, rank, width = down_panels.shape
    chips = blocks // 2
    requests = 2 * blocks
    pooled = groups > 1 and width % (128 * chips * groups) == 0
    caps = [c for c in GROUP_CAPACITIES if c < 2 * held] + [2 * held]
    pool_caps = [c for c in POOL_CAPACITIES if c < 2 * held] + [2 * held] if pooled else caps

    where = jnp.stack([lax.axis_index("groups"), lax.axis_index("blk")]).astype(jnp.int32)
    copies = jnp.broadcast_to(routes.reshape(1, 1, 2), (groups * blocks, 1, 2))
    routes_all = lax.all_to_all(copies, ("groups", "blk"), 0, 0, tiled=True)
    sizes = (2 * held + 1, 2 * requests * (groups if pooled else 1), 2 * requests, requests, held + 1, 1, 1)
    src, pool, slot, count, final, pool_branch, branch = pl.pallas_call(
        functools.partial(tables_kernel, (groups, blocks, held, pooled), pool_caps, caps),
        out_shape=tuple(jax.ShapeDtypeStruct((n,), jnp.int32) for n in sizes),
        in_specs=[SMEM, SMEM],
        out_specs=(SMEM,) * len(sizes),
        scratch_shapes=[pltpu.SMEM((n,), jnp.int32) for n in (blocks * held, chips, blocks * held, chips, blocks * held)],
        name="tables",
    )(where, routes_all)

    panels = lax.switch(
        pool_branch[0],
        [functools.partial(fetch, c, ("groups", "blk") if pooled else "blk", pooled, blocks) for c in pool_caps],
        where, src, pool, down_panels, up_panels,
    )
    terms = pl.pallas_call(
        functools.partial(terms_kernel, blocks),
        out_shape=jax.ShapeDtypeStruct((blocks, 2, rank, width // chips), BF16),
        in_specs=[SMEM, HBM, HBM, VMEM],
        out_specs=ANY,
        scratch_shapes=[
            pltpu.VMEM(activations.shape, BF16),
            pltpu.VMEM(out_grad.shape, BF16),
            pltpu.VMEM((blocks, 2, rank, width // chips), BF16),
            DMA((panels.shape[0] // 2, 2)),
            DMA((chips,)),
        ],
        name="terms",
    )(gates, activations, out_grad, panels)
    terms = lax.all_to_all(terms, "blk", 0, 0, tiled=True)
    return lax.switch(
        branch[0],
        [functools.partial(give_back, c, blocks, held) for c in caps],
        where, slot, count, final, terms,
    )


def solution(mesh):
    in_specs = (
        P(("groups", "blk"), None),
        P(("groups", "blk"), None),
        P("blk", None, None),
        P("blk", None, None),
        P(("groups", "blk"), None),
        P(("groups", "blk"), None),
    )
    out_specs = (P(("groups", "blk"), None, None), P(("groups", "blk"), None, None))
    body = functools.partial(shards, mesh.shape["groups"], mesh.shape["blk"])
    return jax.shard_map(body, mesh=mesh, in_specs=in_specs, out_specs=out_specs, check_vma=False)
```

```python
import functools

import jax
import jax.numpy as jnp
from jax import lax
from jax.experimental import pallas as pl
from jax.experimental.pallas import tpu as pltpu
from jax.sharding import PartitionSpec as P

ANY = pl.BlockSpec(memory_space=pl.ANY)
HBM = pl.BlockSpec(memory_space=pltpu.HBM)
SMEM = pl.BlockSpec(memory_space=pltpu.SMEM)
VMEM = pl.BlockSpec(memory_space=pltpu.VMEM)
DMA = pltpu.SemaphoreType.DMA
BF16 = jnp.bfloat16
GROUP_CAPACITIES = (6, 7, 8, 9, 10)
POOL_CAPACITIES = (9, 10, 11, 12, 13, 15)


def room_for(elements):
    return pltpu.CompilerParams(vmem_limit_bytes=2 * elements + (3 << 20))


def repeat(n, body):
    def step(i, carry):
        body(i)
        return carry

    lax.fori_loop(0, n, step, 0)


def branch_of(most, caps):
    return sum((most > c).astype(jnp.int32) for c in caps[:-1])


def tables_kernel(shape, pool_caps, caps, where_ref, routes_ref, src_ref, pool_ref, slot_ref, count_ref, final_ref, pool_branch_ref, branch_ref, pool_seen, pool_load, seen, load, origin):
    groups, blocks, held, pooled = shape
    requests = 2 * blocks
    chips = blocks // 2
    group, me = where_ref[0], where_ref[1]
    chip = lax.div(me, 2)
    zero = jnp.int32(0)

    def clear(ref, n, value):
        def body(i):
            ref[i] = value

        repeat(n, body)

    def rank_of(seen, load, adapter, owner):
        before = seen[adapter]
        new = before < 0
        filled = load[owner]
        rank = jnp.where(new, filled, before)
        seen[adapter] = rank
        filled = filled + new.astype(jnp.int32)
        load[owner] = filled
        return rank, new, filled

    clear(src_ref, 2 * held, -1)
    clear(final_ref, held, -1)
    clear(pool_load, chips, 0)

    def scan(g, most, mine):
        clear(load, chips, 0)

        def unsee(b):
            for k in range(2):
                adapter = routes_ref[g * blocks + b, 0, k]
                seen[adapter] = -1

        repeat(blocks, unsee)

        def visit(b, most):
            most, pool_most = most
            for k in range(2):
                i = 2 * b + k
                adapter = routes_ref[g * blocks + b, 0, k]
                owner = lax.div(adapter, 2 * held)
                rank, new, filled = rank_of(seen, load, adapter, owner)
                most = jnp.maximum(most, filled)
                if pooled:
                    pool_rank, _, filled = rank_of(pool_seen, pool_load, adapter, owner)
                    pool_most = jnp.maximum(pool_most, filled)
                    at = 2 * (g * requests + i)
                else:
                    pool_rank, at = rank, 2 * i
                if pooled or mine:
                    pool_ref[at] = owner
                    pool_ref[at + 1] = pool_rank
                    src_ref[jnp.where(owner == chip, pool_rank, 2 * held)] = adapter - owner * (2 * held)
                if mine:
                    slot_ref[2 * i] = owner
                    slot_ref[2 * i + 1] = rank
                    count_ref[i] = 0
                    start = jnp.where(new, i, origin[adapter])
                    origin[adapter] = start
                    count_ref[start] = count_ref[start] + 1
                    final_ref[jnp.where(lax.div(adapter, held) == me, adapter - me * held, held)] = rank
            return most, pool_most

        return lax.fori_loop(0, blocks, visit, most)

    if pooled:

        def unsee(b):
            for k in range(2):
                pool_seen[routes_ref[b, 0, k]] = -1

        repeat(groups * blocks, unsee)
    most = scan(group, (zero, zero), True)
    most, pool_most = lax.fori_loop(0, groups - 1, lambda g, m: scan(jnp.where(g < group, g, g + 1), m, False), most)
    pool_branch_ref[0] = branch_of(pool_most if pooled else most, pool_caps)
    branch_ref[0] = branch_of(most, caps)


def take_slots(held, core, src_ref, cap, near, act):
    def visit(c):
        adapter = src_ref[c]

        @pl.when((adapter >= 0) & ((lax.div(adapter, held) == core) == near))
        def _():
            act(c, lax.rem(adapter, held))

    repeat(cap, visit)


def hand_over_kernel(cap, held, pooled, where_ref, src_ref, down_ref, up_ref, send_ref, keep_ref, sems):
    wide = send_ref.shape[2]
    core = lax.rem(where_ref[1], 2)
    columns = pl.ds(pl.multiple_of(where_ref[0] * wide, 128) if pooled else 0, wide)

    def each(do):
        for swap in range(2):

            @pl.when(core == swap)
            def _(swap=swap):
                kept, sent = (up_ref, down_ref) if swap else (down_ref, up_ref)

                def act(c, a):
                    do(pltpu.make_async_copy(sent.at[a, :, columns], send_ref.at[c], sems.at[c, 0]))
                    do(pltpu.make_async_copy(kept.at[a, :, columns], keep_ref.at[c], sems.at[c, 1]))

                take_slots(held, core, src_ref, cap, True, act)

    each(lambda copy: copy.start())
    each(lambda copy: copy.wait())


def cut_kernel(cap, held, chips, where_ref, src_ref, keep_ref, other_ref, out_ref):
    part = out_ref.shape[3]
    core = lax.rem(where_ref[1], 2)
    for near, ref in ((True, keep_ref), (False, other_ref)):

        def act(c, a, ref=ref):
            for p in range(chips):
                out_ref[p, c] = ref[c, :, p * part : (p + 1) * part]

        take_slots(held, core, src_ref, cap, near, act)


def pick_kernel(cap, pool_ref, held_ref, out_ref):
    def visit(i):
        out_ref[i] = held_ref[pool_ref[2 * i] * cap + pool_ref[2 * i + 1]]

    repeat(out_ref.shape[0], visit)


def terms_kernel(blocks, gates_ref, rows_ref, grads_ref, panels_ref, out_ref):
    devices, slots, rank, part = panels_ref.shape
    tokens = rows_ref.shape[0]
    last = (((1,), (1,)), ((), ()))

    def gather(s, sums):
        low, back = sums
        cols = pl.ds(pl.multiple_of(s * part, 128), part)
        down = panels_ref[2 * s].reshape(slots * rank, part)
        up = panels_ref[2 * s + 1].reshape(slots * rank, part)
        low += lax.dot_general(down, rows_ref[:, cols], last, preferred_element_type=jnp.float32)
        back += lax.dot_general(up, grads_ref[:, cols], last, preferred_element_type=jnp.float32)
        return low, back

    zero = jnp.zeros((slots * rank, tokens), jnp.float32)
    low, back = lax.fori_loop(0, devices // 2, gather, (zero, zero), unroll=4)
    low, back = low.astype(BF16), back.astype(BF16)
    wide = out_ref.shape[3]

    def spread(p, carry):
        cols = pl.ds(pl.multiple_of(p * wide, 128), wide)
        down = jnp.dot(back, rows_ref[:, cols], preferred_element_type=jnp.float32)
        up = jnp.dot(low, grads_ref[:, cols], preferred_element_type=jnp.float32)
        for k in range(slots):
            gate = gates_ref[0, k]
            out_ref[2 * p, k] = (down[k * rank : (k + 1) * rank] * gate).astype(out_ref.dtype)
            out_ref[2 * p + 1, k] = (up[k * rank : (k + 1) * rank] * gate).astype(out_ref.dtype)
        return carry

    lax.fori_loop(0, blocks // 2, spread, 0, unroll=2)


def merge_kernel(cap, slot_ref, count_ref, terms_ref, out_ref, total):
    requests = terms_ref.shape[0]

    def slot(i):
        return slot_ref[2 * i] * cap + slot_ref[2 * i + 1]

    def visit(i):
        @pl.when(count_ref[i] == 1)
        def _():
            out_ref[slot(i)] = terms_ref[i]

        @pl.when(count_ref[i] > 1)
        def _():
            s = slot(i)
            total[...] = terms_ref[i].astype(jnp.float32)

            def add(j, _):
                @pl.when(slot(j) == s)
                def _():
                    total[...] += terms_ref[j].astype(jnp.float32)

                return 0

            lax.fori_loop(i + 1, requests, add, 0)
            out_ref[s] = total[...].astype(out_ref.dtype)

    repeat(requests, visit)


def zeros_kernel(down_ref, up_ref, zero, sems):
    held = down_ref.shape[0]
    zero[...] = jnp.zeros_like(zero)

    def each(act):
        def visit(a):
            act(pltpu.make_async_copy(zero, down_ref.at[a], sems.at[a, 0]))
            act(pltpu.make_async_copy(zero, up_ref.at[a], sems.at[a, 1]))

        repeat(held, visit)

    each(lambda copy: copy.start())
    each(lambda copy: copy.wait())


def home_kernel(chips, own, where_ref, final_ref, slices_ref, down_in_ref, up_in_ref, down_ref, up_ref, sems):
    held = down_ref.shape[0]
    part = slices_ref.shape[3]
    core = lax.rem(where_ref[1], 2)
    kind = core if own else 1 - core

    def each(do):
        def visit(a):
            slot = final_ref[a]
            for k, ref in ((0, down_ref), (1, up_ref)):

                @pl.when((slot >= 0) & (kind == k))
                def _(ref=ref):
                    for p in range(chips):
                        do(pltpu.make_async_copy(slices_ref.at[p, slot], ref.at[a, :, pl.ds(p * part, part)], sems.at[a, p]))

        repeat(held, visit)

    each(lambda copy: copy.start())
    each(lambda copy: copy.wait())


def fetch(cap, axes, pooled, blocks, where, src, pool, down_panels, up_panels, activations, out_grad, gates):
    held, rank, width = down_panels.shape
    chips = blocks // 2
    requests = pool.shape[0] // 2
    part = width // (chips * (requests // (2 * blocks)))
    same_core = [[2 * i + c for i in range(chips)] for c in range(2)]
    wide = part * chips
    panel = jax.ShapeDtypeStruct((cap, rank, wide), BF16)
    send, keep = pl.pallas_call(
        functools.partial(hand_over_kernel, cap, held, pooled),
        out_shape=(panel, panel),
        in_specs=[SMEM, SMEM, HBM, HBM],
        out_specs=(VMEM, VMEM),
        scratch_shapes=[DMA((cap, 2))],
        compiler_params=room_for(2 * cap * rank * wide),
        name="hand_over",
    )(where, src, down_panels, up_panels)
    other = lax.ppermute(send, "blk", [(i, i ^ 1) for i in range(blocks)])
    slices = pl.pallas_call(
        functools.partial(cut_kernel, cap, held, chips),
        out_shape=jax.ShapeDtypeStruct((chips, cap, rank, part), BF16),
        in_specs=[SMEM, SMEM, VMEM, VMEM],
        out_specs=VMEM,
        compiler_params=room_for(3 * cap * rank * wide),
        name="cut",
    )(where, src, keep, other)
    slices = lax.all_to_all(slices, "blk", 0, 0, tiled=True, axis_index_groups=same_core)
    picked = pl.pallas_call(
        functools.partial(pick_kernel, cap),
        out_shape=jax.ShapeDtypeStruct((requests, rank, part), BF16),
        in_specs=[SMEM, VMEM],
        out_specs=VMEM,
        compiler_params=room_for((chips * cap + requests) * rank * part),
        name="pick",
    )(pool, slices.reshape(chips * cap, rank, part))
    panels = lax.all_to_all(picked.reshape(requests // 2, 2, rank, part), axes, 0, 0, tiled=True)
    return pl.pallas_call(
        functools.partial(terms_kernel, blocks),
        out_shape=jax.ShapeDtypeStruct((blocks, 2, rank, width // chips), BF16),
        in_specs=[SMEM, VMEM, VMEM, VMEM],
        out_specs=VMEM,
        compiler_params=room_for(2 * out_grad.size + 2 * panels.size),
        name="terms",
    )(gates, activations, out_grad, panels)


def give_back(cap, blocks, held, where, slot, count, final, terms):
    _, _, rank, part = terms.shape
    chips = blocks // 2
    width = part * chips
    partner = [(i, i ^ 1) for i in range(blocks)]
    same_core = [[2 * i + c for i in range(chips)] for c in range(2)]
    terms = lax.all_to_all(terms, "blk", 0, 0, tiled=True)
    shape = jax.ShapeDtypeStruct((held, rank, width), BF16)
    grads = pl.pallas_call(
        zeros_kernel,
        out_shape=(shape, shape),
        in_specs=[],
        out_specs=(ANY, ANY),
        scratch_shapes=[pltpu.VMEM((rank, width), BF16), DMA((held, 2))],
        cost_estimate=pl.CostEstimate(flops=0, bytes_accessed=4 * held * rank * width, transcendentals=0),
        name="zeros",
    )()
    terms, grads = lax.optimization_barrier((terms, grads))
    sums = pl.pallas_call(
        functools.partial(merge_kernel, cap),
        out_shape=jax.ShapeDtypeStruct((chips * cap, rank, part), BF16),
        in_specs=[SMEM, SMEM, VMEM],
        out_specs=VMEM,
        scratch_shapes=[pltpu.VMEM((rank, part), jnp.float32)],
        compiler_params=room_for(terms.size + (chips * cap + 2) * rank * part),
        name="merge",
    )(slot, count, terms.reshape(2 * blocks, rank, part))
    own = lax.all_to_all(sums.reshape(chips, cap, rank, part), "blk", 0, 0, tiled=True, axis_index_groups=same_core)
    other = lax.ppermute(own, "blk", partner)
    for mine, slices in ((True, own), (False, other)):
        grads = pl.pallas_call(
            functools.partial(home_kernel, chips, mine),
            out_shape=(shape, shape),
            in_specs=[SMEM, SMEM, VMEM, ANY, ANY],
            out_specs=(ANY, ANY),
            scratch_shapes=[DMA((held, chips))],
            input_output_aliases={3: 0, 4: 1},
            cost_estimate=pl.CostEstimate(flops=0, bytes_accessed=4 * own.size, transcendentals=0),
            compiler_params=room_for(own.size),
            name="home_own" if mine else "home_other",
        )(where, final, slices, *grads)
    return grads


def shards(groups, blocks, activations, out_grad, down_panels, up_panels, routes, gates):
    held, rank, width = down_panels.shape
    chips = blocks // 2
    requests = 2 * blocks
    pooled = groups > 1 and width % (128 * chips * groups) == 0
    caps = [c for c in GROUP_CAPACITIES if c < 2 * held] + [2 * held]
    pool_caps = [c for c in POOL_CAPACITIES if c < 2 * held] + [2 * held] if pooled else caps

    where = jnp.stack([lax.axis_index("groups"), lax.axis_index("blk")]).astype(jnp.int32)
    copies = jnp.broadcast_to(routes.reshape(1, 1, 2), (groups * blocks, 1, 2))
    routes_all = lax.all_to_all(copies, ("groups", "blk"), 0, 0, tiled=True)
    sizes = (2 * held + 1, 2 * requests * (groups if pooled else 1), 2 * requests, requests, held + 1, 1, 1)
    src, pool, slot, count, final, pool_branch, branch = pl.pallas_call(
        functools.partial(tables_kernel, (groups, blocks, held, pooled), pool_caps, caps),
        out_shape=tuple(jax.ShapeDtypeStruct((n,), jnp.int32) for n in sizes),
        in_specs=[SMEM, SMEM],
        out_specs=(SMEM,) * len(sizes),
        scratch_shapes=[pltpu.SMEM((n,), jnp.int32) for n in (blocks * held, chips, blocks * held, chips, blocks * held)],
        name="tables",
    )(where, routes_all)

    terms = lax.switch(
        pool_branch[0],
        [functools.partial(fetch, c, ("groups", "blk") if pooled else "blk", pooled, blocks) for c in pool_caps],
        where, src, pool, down_panels, up_panels, activations, out_grad, gates,
    )
    return lax.switch(
        branch[0],
        [functools.partial(give_back, c, blocks, held) for c in caps],
        where, slot, count, final, terms,
    )


def solution(mesh):
    in_specs = (
        P(("groups", "blk"), None),
        P(("groups", "blk"), None),
        P("blk", None, None),
        P("blk", None, None),
        P(("groups", "blk"), None),
        P(("groups", "blk"), None),
    )
    out_specs = (P(("groups", "blk"), None, None), P(("groups", "blk"), None, None))
    body = functools.partial(shards, mesh.shape["groups"], mesh.shape["blk"])
    return jax.shard_map(body, mesh=mesh, in_specs=in_specs, out_specs=out_specs, check_vma=False)
```

```python
import functools

import jax
import jax.numpy as jnp
from jax import lax
from jax.experimental import pallas as pl
from jax.experimental.pallas import tpu as pltpu
from jax.sharding import PartitionSpec as P

ANY = pl.BlockSpec(memory_space=pl.ANY)
HBM = pl.BlockSpec(memory_space=pltpu.HBM)
SMEM = pl.BlockSpec(memory_space=pltpu.SMEM)
VMEM = pl.BlockSpec(memory_space=pltpu.VMEM)
DMA = pltpu.SemaphoreType.DMA
BF16 = jnp.bfloat16
GROUP_CAPACITIES = (5, 6, 7, 8, 9, 10)
POOL_CAPACITIES = (8, 9, 10, 11, 12, 13, 14, 16)


def room_for(elements):
    return pltpu.CompilerParams(vmem_limit_bytes=2 * elements + (3 << 20))


def repeat(n, body, unroll=1):
    def step(i, carry):
        body(i)
        return carry

    lax.fori_loop(0, n, step, 0, unroll=unroll)


def branch_of(most, caps):
    return sum((most > c).astype(jnp.int32) for c in caps[:-1])


def tables_kernel(shape, pool_caps, caps, where_ref, routes_ref, src_ref, pool_ref, slot_ref, count_ref, final_ref, pool_branch_ref, branch_ref, pool_seen, pool_load, seen, load, origin):
    groups, blocks, held, pooled = shape
    requests = 2 * blocks
    chips = blocks // 2
    group, me = where_ref[0], where_ref[1]
    chip = lax.div(me, 2)
    zero = jnp.int32(0)

    def clear(ref, n, value):
        def body(i):
            ref[i] = value

        repeat(n, body, 8 if n % 8 == 0 else 4)

    def rank_of(seen, load, adapter, owner):
        before = seen[adapter]
        new = before < 0
        filled = load[owner]
        rank = jnp.where(new, filled, before)
        seen[adapter] = rank
        filled = filled + new.astype(jnp.int32)
        load[owner] = filled
        return rank, new, filled

    clear(src_ref, 2 * held, -1)
    clear(final_ref, held, -1)
    clear(pool_load, chips, 0)

    def scan(g, most, mine):
        clear(load, chips, 0)

        def unsee(b):
            for k in range(2):
                adapter = routes_ref[g * blocks + b, 0, k]
                seen[adapter] = -1

        repeat(blocks, unsee, 8)

        def visit(b, most):
            most, pool_most = most
            for k in range(2):
                i = 2 * b + k
                adapter = routes_ref[g * blocks + b, 0, k]
                owner = lax.div(adapter, 2 * held)
                rank, new, filled = rank_of(seen, load, adapter, owner)
                most = jnp.maximum(most, filled)
                if pooled:
                    pool_rank, _, filled = rank_of(pool_seen, pool_load, adapter, owner)
                    pool_most = jnp.maximum(pool_most, filled)
                    at = 2 * (g * requests + i)
                else:
                    pool_rank, at = rank, 2 * i
                if pooled or mine:
                    pool_ref[at] = owner
                    pool_ref[at + 1] = pool_rank
                    src_ref[jnp.where(owner == chip, pool_rank, 2 * held)] = adapter - owner * (2 * held)
                if mine:
                    slot_ref[2 * i] = owner
                    slot_ref[2 * i + 1] = rank
                    count_ref[i] = 0
                    start = jnp.where(new, i, origin[adapter])
                    origin[adapter] = start
                    count_ref[start] = count_ref[start] + 1
                    final_ref[jnp.where(lax.div(adapter, held) == me, adapter - me * held, held)] = rank
            return most, pool_most

        return lax.fori_loop(0, blocks, visit, most, unroll=4)

    if pooled:

        def unsee(b):
            for k in range(2):
                pool_seen[routes_ref[b, 0, k]] = -1

        repeat(groups * blocks, unsee, 8)
    most = scan(group, (zero, zero), True)
    most, pool_most = lax.fori_loop(0, groups - 1, lambda g, m: scan(jnp.where(g < group, g, g + 1), m, False), most)
    pool_branch_ref[0] = branch_of(pool_most if pooled else most, pool_caps)
    branch_ref[0] = branch_of(most, caps)


def take_slots(held, core, src_ref, cap, near, act):
    def visit(c):
        adapter = src_ref[c]

        @pl.when((adapter >= 0) & ((lax.div(adapter, held) == core) == near))
        def _():
            act(c, lax.rem(adapter, held))

    repeat(cap, visit)


def hand_over_kernel(cap, held, pooled, where_ref, src_ref, down_ref, up_ref, send_ref, keep_ref, sems):
    wide = send_ref.shape[2]
    core = lax.rem(where_ref[1], 2)
    columns = pl.ds(pl.multiple_of(where_ref[0] * wide, 128) if pooled else 0, wide)

    def each(do):
        for swap in range(2):

            @pl.when(core == swap)
            def _(swap=swap):
                kept, sent = (up_ref, down_ref) if swap else (down_ref, up_ref)

                def act(c, a):
                    do(pltpu.make_async_copy(sent.at[a, :, columns], send_ref.at[c], sems.at[c, 0]))
                    do(pltpu.make_async_copy(kept.at[a, :, columns], keep_ref.at[c], sems.at[c, 1]))

                take_slots(held, core, src_ref, cap, True, act)

    each(lambda copy: copy.start())
    each(lambda copy: copy.wait())


def cut_kernel(cap, held, chips, where_ref, src_ref, keep_ref, other_ref, out_ref):
    part = out_ref.shape[3]
    core = lax.rem(where_ref[1], 2)
    for near, ref in ((True, keep_ref), (False, other_ref)):

        def act(c, a, ref=ref):
            for p in range(chips):
                out_ref[p, c] = ref[c, :, p * part : (p + 1) * part]

        take_slots(held, core, src_ref, cap, near, act)


def pick_kernel(cap, pool_ref, held_ref, out_ref):
    def visit(i):
        out_ref[i] = held_ref[pool_ref[2 * i] * cap + pool_ref[2 * i + 1]]

    repeat(out_ref.shape[0], visit)


def terms_kernel(blocks, gates_ref, rows_ref, grads_ref, panels_ref, out_ref):
    devices, slots, rank, part = panels_ref.shape
    tokens = rows_ref.shape[0]
    last = (((1,), (1,)), ((), ()))

    def gather(s, sums):
        low, back = sums
        cols = pl.ds(pl.multiple_of(s * part, 128), part)
        down = panels_ref[2 * s].reshape(slots * rank, part)
        up = panels_ref[2 * s + 1].reshape(slots * rank, part)
        low += lax.dot_general(down, rows_ref[:, cols], last, preferred_element_type=jnp.float32)
        back += lax.dot_general(up, grads_ref[:, cols], last, preferred_element_type=jnp.float32)
        return low, back

    zero = jnp.zeros((slots * rank, tokens), jnp.float32)
    low, back = lax.fori_loop(0, devices // 2, gather, (zero, zero), unroll=8)
    low, back = low.astype(BF16), back.astype(BF16)
    wide = out_ref.shape[3]

    def spread(p, carry):
        cols = pl.ds(pl.multiple_of(p * wide, 128), wide)
        down = jnp.dot(back, rows_ref[:, cols], preferred_element_type=jnp.float32)
        up = jnp.dot(low, grads_ref[:, cols], preferred_element_type=jnp.float32)
        for k in range(slots):
            gate = gates_ref[0, k]
            out_ref[2 * p, k] = (down[k * rank : (k + 1) * rank] * gate).astype(out_ref.dtype)
            out_ref[2 * p + 1, k] = (up[k * rank : (k + 1) * rank] * gate).astype(out_ref.dtype)
        return carry

    lax.fori_loop(0, blocks // 2, spread, 0, unroll=4)


def merge_kernel(cap, slot_ref, count_ref, terms_ref, out_ref, total):
    requests = terms_ref.shape[0]

    def slot(i):
        return slot_ref[2 * i] * cap + slot_ref[2 * i + 1]

    def visit(i):
        @pl.when(count_ref[i] == 1)
        def _():
            out_ref[slot(i)] = terms_ref[i]

        @pl.when(count_ref[i] > 1)
        def _():
            s = slot(i)
            total[...] = terms_ref[i].astype(jnp.float32)

            def add(j, _):
                @pl.when(slot(j) == s)
                def _():
                    total[...] += terms_ref[j].astype(jnp.float32)

                return 0

            lax.fori_loop(i + 1, requests, add, 0)
            out_ref[s] = total[...].astype(out_ref.dtype)

    repeat(requests, visit, 4)


def zeros_kernel(down_ref, up_ref, zero, sems):
    held = down_ref.shape[0]
    zero[...] = jnp.zeros_like(zero)

    def each(act):
        def visit(a):
            act(pltpu.make_async_copy(zero, down_ref.at[a], sems.at[a, 0]))
            act(pltpu.make_async_copy(zero, up_ref.at[a], sems.at[a, 1]))

        repeat(held, visit)

    each(lambda copy: copy.start())
    each(lambda copy: copy.wait())


def home_kernel(chips, own, where_ref, final_ref, slices_ref, down_in_ref, up_in_ref, down_ref, up_ref, sems):
    held = down_ref.shape[0]
    part = slices_ref.shape[3]
    core = lax.rem(where_ref[1], 2)
    kind = core if own else 1 - core

    def each(do):
        def visit(a):
            slot = final_ref[a]
            for k, ref in ((0, down_ref), (1, up_ref)):

                @pl.when((slot >= 0) & (kind == k))
                def _(ref=ref):
                    for p in range(chips):
                        do(pltpu.make_async_copy(slices_ref.at[p, slot], ref.at[a, :, pl.ds(p * part, part)], sems.at[a, p]))

        repeat(held, visit)

    each(lambda copy: copy.start())
    each(lambda copy: copy.wait())


def fetch(cap, axes, pooled, blocks, where, src, pool, down_panels, up_panels, activations, out_grad, gates):
    held, rank, width = down_panels.shape
    chips = blocks // 2
    requests = pool.shape[0] // 2
    part = width // (chips * (requests // (2 * blocks)))
    same_core = [[2 * i + c for i in range(chips)] for c in range(2)]
    wide = part * chips
    panel = jax.ShapeDtypeStruct((cap, rank, wide), BF16)
    send, keep = pl.pallas_call(
        functools.partial(hand_over_kernel, cap, held, pooled),
        out_shape=(panel, panel),
        in_specs=[SMEM, SMEM, HBM, HBM],
        out_specs=(VMEM, VMEM),
        scratch_shapes=[DMA((cap, 2))],
        compiler_params=room_for(2 * cap * rank * wide),
        name="hand_over",
    )(where, src, down_panels, up_panels)
    other = lax.ppermute(send, "blk", [(i, i ^ 1) for i in range(blocks)])
    slices = pl.pallas_call(
        functools.partial(cut_kernel, cap, held, chips),
        out_shape=jax.ShapeDtypeStruct((chips, cap, rank, part), BF16),
        in_specs=[SMEM, SMEM, VMEM, VMEM],
        out_specs=VMEM,
        compiler_params=room_for(3 * cap * rank * wide),
        name="cut",
    )(where, src, keep, other)
    slices = lax.all_to_all(slices, "blk", 0, 0, tiled=True, axis_index_groups=same_core)
    picked = pl.pallas_call(
        functools.partial(pick_kernel, cap),
        out_shape=jax.ShapeDtypeStruct((requests, rank, part), BF16),
        in_specs=[SMEM, VMEM],
        out_specs=VMEM,
        compiler_params=room_for((chips * cap + requests) * rank * part),
        name="pick",
    )(pool, slices.reshape(chips * cap, rank, part))
    panels = lax.all_to_all(picked.reshape(requests // 2, 2, rank, part), axes, 0, 0, tiled=True)
    return pl.pallas_call(
        functools.partial(terms_kernel, blocks),
        out_shape=jax.ShapeDtypeStruct((blocks, 2, rank, width // chips), BF16),
        in_specs=[SMEM, VMEM, VMEM, VMEM],
        out_specs=VMEM,
        compiler_params=room_for(2 * out_grad.size + 2 * panels.size),
        name="terms",
    )(gates, activations, out_grad, panels)


def give_back(cap, blocks, held, where, slot, count, final, terms):
    _, _, rank, part = terms.shape
    chips = blocks // 2
    width = part * chips
    partner = [(i, i ^ 1) for i in range(blocks)]
    same_core = [[2 * i + c for i in range(chips)] for c in range(2)]
    terms = lax.all_to_all(terms, "blk", 0, 0, tiled=True)
    shape = jax.ShapeDtypeStruct((held, rank, width), BF16)
    grads = pl.pallas_call(
        zeros_kernel,
        out_shape=(shape, shape),
        in_specs=[],
        out_specs=(ANY, ANY),
        scratch_shapes=[pltpu.VMEM((rank, width), BF16), DMA((held, 2))],
        cost_estimate=pl.CostEstimate(flops=0, bytes_accessed=4 * held * rank * width, transcendentals=0),
        name="zeros",
    )()
    terms, grads = lax.optimization_barrier((terms, grads))
    sums = pl.pallas_call(
        functools.partial(merge_kernel, cap),
        out_shape=jax.ShapeDtypeStruct((chips * cap, rank, part), BF16),
        in_specs=[SMEM, SMEM, VMEM],
        out_specs=VMEM,
        scratch_shapes=[pltpu.VMEM((rank, part), jnp.float32)],
        compiler_params=room_for(terms.size + (chips * cap + 2) * rank * part),
        name="merge",
    )(slot, count, terms.reshape(2 * blocks, rank, part))
    own = lax.all_to_all(sums.reshape(chips, cap, rank, part), "blk", 0, 0, tiled=True, axis_index_groups=same_core)
    other = lax.ppermute(own, "blk", partner)
    for mine, slices in ((True, own), (False, other)):
        grads = pl.pallas_call(
            functools.partial(home_kernel, chips, mine),
            out_shape=(shape, shape),
            in_specs=[SMEM, SMEM, VMEM, ANY, ANY],
            out_specs=(ANY, ANY),
            scratch_shapes=[DMA((held, chips))],
            input_output_aliases={3: 0, 4: 1},
            cost_estimate=pl.CostEstimate(flops=0, bytes_accessed=4 * own.size, transcendentals=0),
            compiler_params=room_for(own.size),
            name="home_own" if mine else "home_other",
        )(where, final, slices, *grads)
    return grads


def shards(groups, blocks, activations, out_grad, down_panels, up_panels, routes, gates):
    held, rank, width = down_panels.shape
    chips = blocks // 2
    requests = 2 * blocks
    pooled = groups > 1 and width % (128 * chips * groups) == 0
    caps = [c for c in GROUP_CAPACITIES if c < 2 * held] + [2 * held]
    pool_caps = [c for c in POOL_CAPACITIES if c < 2 * held] + [2 * held] if pooled else caps

    where = jnp.stack([lax.axis_index("groups"), lax.axis_index("blk")]).astype(jnp.int32)
    copies = jnp.broadcast_to(routes.reshape(1, 1, 2), (groups * blocks, 1, 2))
    routes_all = lax.all_to_all(copies, ("groups", "blk"), 0, 0, tiled=True)
    sizes = (2 * held + 1, 2 * requests * (groups if pooled else 1), 2 * requests, requests, held + 1, 1, 1)
    src, pool, slot, count, final, pool_branch, branch = pl.pallas_call(
        functools.partial(tables_kernel, (groups, blocks, held, pooled), pool_caps, caps),
        out_shape=tuple(jax.ShapeDtypeStruct((n,), jnp.int32) for n in sizes),
        in_specs=[SMEM, SMEM],
        out_specs=(SMEM,) * len(sizes),
        scratch_shapes=[pltpu.SMEM((n,), jnp.int32) for n in (blocks * held, chips, blocks * held, chips, blocks * held)],
        name="tables",
    )(where, routes_all)

    terms = lax.switch(
        pool_branch[0],
        [functools.partial(fetch, c, ("groups", "blk") if pooled else "blk", pooled, blocks) for c in pool_caps],
        where, src, pool, down_panels, up_panels, activations, out_grad, gates,
    )
    return lax.switch(
        branch[0],
        [functools.partial(give_back, c, blocks, held) for c in caps],
        where, slot, count, final, terms,
    )


def solution(mesh):
    in_specs = (
        P(("groups", "blk"), None),
        P(("groups", "blk"), None),
        P("blk", None, None),
        P("blk", None, None),
        P(("groups", "blk"), None),
        P(("groups", "blk"), None),
    )
    out_specs = (P(("groups", "blk"), None, None), P(("groups", "blk"), None, None))
    body = functools.partial(shards, mesh.shape["groups"], mesh.shape["blk"])
    return jax.shard_map(body, mesh=mesh, in_specs=in_specs, out_specs=out_specs, check_vma=False)
```

```python
import functools

import jax
import jax.numpy as jnp
from jax import lax
from jax.experimental import pallas as pl
from jax.experimental.pallas import tpu as pltpu
from jax.sharding import PartitionSpec as P

ANY = pl.BlockSpec(memory_space=pl.ANY)
HBM = pl.BlockSpec(memory_space=pltpu.HBM)
SMEM = pl.BlockSpec(memory_space=pltpu.SMEM)
VMEM = pl.BlockSpec(memory_space=pltpu.VMEM)
DMA = pltpu.SemaphoreType.DMA
BF16 = jnp.bfloat16
GROUP_CAPACITIES = (5, 6, 7, 8, 9, 10)
POOL_CAPACITIES = (8, 9, 10, 11, 12, 13, 14, 15, 16)


def room_for(elements):
    return pltpu.CompilerParams(vmem_limit_bytes=2 * elements + (3 << 20))


def repeat(n, body, unroll=1):
    def step(i, carry):
        body(i)
        return carry

    lax.fori_loop(0, n, step, 0, unroll=unroll)


def branch_of(most, caps):
    return sum((most > c).astype(jnp.int32) for c in caps[:-1])


def tables_kernel(shape, pool_caps, caps, where_ref, routes_ref, src_ref, pool_ref, slot_ref, count_ref, final_ref, pool_branch_ref, branch_ref, pool_seen, pool_load, seen, load, origin):
    groups, blocks, held, pooled = shape
    requests = 2 * blocks
    chips = blocks // 2
    group, me = where_ref[0], where_ref[1]
    chip = lax.div(me, 2)
    zero = jnp.int32(0)

    def clear(ref, n, value):
        def body(i):
            ref[i] = value

        repeat(n, body, 8 if n % 8 == 0 else 4)

    def rank_of(seen, load, adapter, owner):
        before = seen[adapter]
        new = before < 0
        filled = load[owner]
        rank = jnp.where(new, filled, before)
        seen[adapter] = rank
        filled = filled + new.astype(jnp.int32)
        load[owner] = filled
        return rank, new, filled

    clear(src_ref, 2 * held, -1)
    clear(final_ref, held, -1)
    clear(pool_load, chips, 0)

    def scan(g, most, mine):
        clear(load, chips, 0)

        def unsee(b):
            for k in range(2):
                adapter = routes_ref[g * blocks + b, 0, k]
                seen[adapter] = -1

        repeat(blocks, unsee, 8)

        def visit(b, most):
            most, pool_most = most
            for k in range(2):
                i = 2 * b + k
                adapter = routes_ref[g * blocks + b, 0, k]
                owner = lax.div(adapter, 2 * held)
                rank, new, filled = rank_of(seen, load, adapter, owner)
                most = jnp.maximum(most, filled)
                if pooled:
                    pool_rank, _, filled = rank_of(pool_seen, pool_load, adapter, owner)
                    pool_most = jnp.maximum(pool_most, filled)
                    at = 2 * (g * requests + i)
                else:
                    pool_rank, at = rank, 2 * i
                if pooled or mine:
                    pool_ref[at] = owner
                    pool_ref[at + 1] = pool_rank
                    src_ref[jnp.where(owner == chip, pool_rank, 2 * held)] = adapter - owner * (2 * held)
                if mine:
                    slot_ref[2 * i] = owner
                    slot_ref[2 * i + 1] = rank
                    count_ref[i] = 0
                    start = jnp.where(new, i, origin[adapter])
                    origin[adapter] = start
                    count_ref[start] = count_ref[start] + 1
                    final_ref[jnp.where(lax.div(adapter, held) == me, adapter - me * held, held)] = rank
            return most, pool_most

        return lax.fori_loop(0, blocks, visit, most, unroll=8)

    if pooled:

        def unsee(b):
            for k in range(2):
                pool_seen[routes_ref[b, 0, k]] = -1

        repeat(groups * blocks, unsee, 8)
    most = scan(group, (zero, zero), True)
    most, pool_most = lax.fori_loop(0, groups - 1, lambda g, m: scan(jnp.where(g < group, g, g + 1), m, False), most)
    pool_branch_ref[0] = branch_of(pool_most if pooled else most, pool_caps)
    branch_ref[0] = branch_of(most, caps)


def take_slots(held, core, src_ref, cap, near, act):
    def visit(c):
        adapter = src_ref[c]

        @pl.when((adapter >= 0) & ((lax.div(adapter, held) == core) == near))
        def _():
            act(c, lax.rem(adapter, held))

    repeat(cap, visit)


def hand_over_kernel(cap, held, pooled, where_ref, src_ref, down_ref, up_ref, send_ref, keep_ref, sems):
    wide = send_ref.shape[2]
    core = lax.rem(where_ref[1], 2)
    columns = pl.ds(pl.multiple_of(where_ref[0] * wide, 128) if pooled else 0, wide)

    def each(do):
        for swap in range(2):

            @pl.when(core == swap)
            def _(swap=swap):
                kept, sent = (up_ref, down_ref) if swap else (down_ref, up_ref)

                def act(c, a):
                    do(pltpu.make_async_copy(sent.at[a, :, columns], send_ref.at[c], sems.at[c, 0]))
                    do(pltpu.make_async_copy(kept.at[a, :, columns], keep_ref.at[c], sems.at[c, 1]))

                take_slots(held, core, src_ref, cap, True, act)

    each(lambda copy: copy.start())
    each(lambda copy: copy.wait())


def cut_kernel(cap, held, chips, where_ref, src_ref, keep_ref, other_ref, out_ref):
    part = out_ref.shape[3]
    core = lax.rem(where_ref[1], 2)
    for near, ref in ((True, keep_ref), (False, other_ref)):

        def act(c, a, ref=ref):
            for p in range(chips):
                out_ref[p, c] = ref[c, :, p * part : (p + 1) * part]

        take_slots(held, core, src_ref, cap, near, act)


def pick_kernel(cap, pool_ref, held_ref, out_ref):
    def visit(i):
        out_ref[i] = held_ref[pool_ref[2 * i] * cap + pool_ref[2 * i + 1]]

    repeat(out_ref.shape[0], visit)


def terms_kernel(blocks, gates_ref, rows_ref, grads_ref, panels_ref, out_ref):
    devices, slots, rank, part = panels_ref.shape
    tokens = rows_ref.shape[0]
    last = (((1,), (1,)), ((), ()))

    def gather(s, sums):
        low, back = sums
        cols = pl.ds(pl.multiple_of(s * part, 128), part)
        down = panels_ref[2 * s].reshape(slots * rank, part)
        up = panels_ref[2 * s + 1].reshape(slots * rank, part)
        low += lax.dot_general(down, rows_ref[:, cols], last, preferred_element_type=jnp.float32)
        back += lax.dot_general(up, grads_ref[:, cols], last, preferred_element_type=jnp.float32)
        return low, back

    zero = jnp.zeros((slots * rank, tokens), jnp.float32)
    low, back = lax.fori_loop(0, devices // 2, gather, (zero, zero), unroll=8)
    low, back = low.astype(BF16), back.astype(BF16)
    wide = out_ref.shape[3]

    def spread(p, carry):
        cols = pl.ds(pl.multiple_of(p * wide, 128), wide)
        down = jnp.dot(back, rows_ref[:, cols], preferred_element_type=jnp.float32)
        up = jnp.dot(low, grads_ref[:, cols], preferred_element_type=jnp.float32)
        for k in range(slots):
            gate = gates_ref[0, k]
            out_ref[2 * p, k] = (down[k * rank : (k + 1) * rank] * gate).astype(out_ref.dtype)
            out_ref[2 * p + 1, k] = (up[k * rank : (k + 1) * rank] * gate).astype(out_ref.dtype)
        return carry

    lax.fori_loop(0, blocks // 2, spread, 0, unroll=8)


def merge_kernel(cap, slot_ref, count_ref, terms_ref, out_ref, total):
    requests = terms_ref.shape[0]

    def slot(i):
        return slot_ref[2 * i] * cap + slot_ref[2 * i + 1]

    def visit(i):
        @pl.when(count_ref[i] == 1)
        def _():
            out_ref[slot(i)] = terms_ref[i]

        @pl.when(count_ref[i] > 1)
        def _():
            s = slot(i)
            total[...] = terms_ref[i].astype(jnp.float32)

            def add(j, _):
                @pl.when(slot(j) == s)
                def _():
                    total[...] += terms_ref[j].astype(jnp.float32)

                return 0

            lax.fori_loop(i + 1, requests, add, 0)
            out_ref[s] = total[...].astype(out_ref.dtype)

    repeat(requests, visit, 4)


def zeros_kernel(down_ref, up_ref, zero, sems):
    held = down_ref.shape[0]
    zero[...] = jnp.zeros_like(zero)

    def each(act):
        def visit(a):
            act(pltpu.make_async_copy(zero, down_ref.at[a], sems.at[a, 0]))
            act(pltpu.make_async_copy(zero, up_ref.at[a], sems.at[a, 1]))

        repeat(held, visit)

    each(lambda copy: copy.start())
    each(lambda copy: copy.wait())


def home_kernel(chips, own, where_ref, final_ref, slices_ref, down_in_ref, up_in_ref, down_ref, up_ref, sems):
    held = down_ref.shape[0]
    part = slices_ref.shape[3]
    core = lax.rem(where_ref[1], 2)
    kind = core if own else 1 - core

    def each(do):
        def visit(a):
            slot = final_ref[a]
            for k, ref in ((0, down_ref), (1, up_ref)):

                @pl.when((slot >= 0) & (kind == k))
                def _(ref=ref):
                    for p in range(chips):
                        do(pltpu.make_async_copy(slices_ref.at[p, slot], ref.at[a, :, pl.ds(p * part, part)], sems.at[a, p]))

        repeat(held, visit)

    each(lambda copy: copy.start())
    each(lambda copy: copy.wait())


def fetch(cap, axes, pooled, blocks, where, src, pool, down_panels, up_panels, activations, out_grad, gates):
    held, rank, width = down_panels.shape
    chips = blocks // 2
    requests = pool.shape[0] // 2
    part = width // (chips * (requests // (2 * blocks)))
    same_core = [[2 * i + c for i in range(chips)] for c in range(2)]
    wide = part * chips
    panel = jax.ShapeDtypeStruct((cap, rank, wide), BF16)
    send, keep = pl.pallas_call(
        functools.partial(hand_over_kernel, cap, held, pooled),
        out_shape=(panel, panel),
        in_specs=[SMEM, SMEM, HBM, HBM],
        out_specs=(VMEM, VMEM),
        scratch_shapes=[DMA((cap, 2))],
        compiler_params=room_for(2 * cap * rank * wide),
        name="hand_over",
    )(where, src, down_panels, up_panels)
    other = lax.ppermute(send, "blk", [(i, i ^ 1) for i in range(blocks)])
    slices = pl.pallas_call(
        functools.partial(cut_kernel, cap, held, chips),
        out_shape=jax.ShapeDtypeStruct((chips, cap, rank, part), BF16),
        in_specs=[SMEM, SMEM, VMEM, VMEM],
        out_specs=VMEM,
        compiler_params=room_for(3 * cap * rank * wide),
        name="cut",
    )(where, src, keep, other)
    slices = lax.all_to_all(slices, "blk", 0, 0, tiled=True, axis_index_groups=same_core)
    picked = pl.pallas_call(
        functools.partial(pick_kernel, cap),
        out_shape=jax.ShapeDtypeStruct((requests, rank, part), BF16),
        in_specs=[SMEM, VMEM],
        out_specs=VMEM,
        compiler_params=room_for((chips * cap + requests) * rank * part),
        name="pick",
    )(pool, slices.reshape(chips * cap, rank, part))
    panels = lax.all_to_all(picked.reshape(requests // 2, 2, rank, part), axes, 0, 0, tiled=True)
    return pl.pallas_call(
        functools.partial(terms_kernel, blocks),
        out_shape=jax.ShapeDtypeStruct((blocks, 2, rank, width // chips), BF16),
        in_specs=[SMEM, VMEM, VMEM, VMEM],
        out_specs=VMEM,
        compiler_params=room_for(2 * out_grad.size + 2 * panels.size),
        name="terms",
    )(gates, activations, out_grad, panels)


def give_back(cap, blocks, held, where, slot, count, final, terms):
    _, _, rank, part = terms.shape
    chips = blocks // 2
    width = part * chips
    partner = [(i, i ^ 1) for i in range(blocks)]
    same_core = [[2 * i + c for i in range(chips)] for c in range(2)]
    terms = lax.all_to_all(terms, "blk", 0, 0, tiled=True)
    shape = jax.ShapeDtypeStruct((held, rank, width), BF16)
    grads = pl.pallas_call(
        zeros_kernel,
        out_shape=(shape, shape),
        in_specs=[],
        out_specs=(ANY, ANY),
        scratch_shapes=[pltpu.VMEM((rank, width), BF16), DMA((held, 2))],
        cost_estimate=pl.CostEstimate(flops=0, bytes_accessed=4 * held * rank * width, transcendentals=0),
        name="zeros",
    )()
    terms, grads = lax.optimization_barrier((terms, grads))
    sums = pl.pallas_call(
        functools.partial(merge_kernel, cap),
        out_shape=jax.ShapeDtypeStruct((chips * cap, rank, part), BF16),
        in_specs=[SMEM, SMEM, VMEM],
        out_specs=VMEM,
        scratch_shapes=[pltpu.VMEM((rank, part), jnp.float32)],
        compiler_params=room_for(terms.size + (chips * cap + 2) * rank * part),
        name="merge",
    )(slot, count, terms.reshape(2 * blocks, rank, part))
    own = lax.all_to_all(sums.reshape(chips, cap, rank, part), "blk", 0, 0, tiled=True, axis_index_groups=same_core)
    other = lax.ppermute(own, "blk", partner)
    for mine, slices in ((True, own), (False, other)):
        grads = pl.pallas_call(
            functools.partial(home_kernel, chips, mine),
            out_shape=(shape, shape),
            in_specs=[SMEM, SMEM, VMEM, ANY, ANY],
            out_specs=(ANY, ANY),
            scratch_shapes=[DMA((held, chips))],
            input_output_aliases={3: 0, 4: 1},
            cost_estimate=pl.CostEstimate(flops=0, bytes_accessed=4 * own.size, transcendentals=0),
            compiler_params=room_for(own.size),
            name="home_own" if mine else "home_other",
        )(where, final, slices, *grads)
    return grads


def shards(groups, blocks, activations, out_grad, down_panels, up_panels, routes, gates):
    held, rank, width = down_panels.shape
    chips = blocks // 2
    requests = 2 * blocks
    pooled = groups > 1 and width % (128 * chips * groups) == 0
    caps = [c for c in GROUP_CAPACITIES if c < 2 * held] + [2 * held]
    pool_caps = [c for c in POOL_CAPACITIES if c < 2 * held] + [2 * held] if pooled else caps

    where = jnp.stack([lax.axis_index("groups"), lax.axis_index("blk")]).astype(jnp.int32)
    copies = jnp.broadcast_to(routes.reshape(1, 1, 2), (groups * blocks, 1, 2))
    routes_all = lax.all_to_all(copies, ("groups", "blk"), 0, 0, tiled=True)
    sizes = (2 * held + 1, 2 * requests * (groups if pooled else 1), 2 * requests, requests, held + 1, 1, 1)
    src, pool, slot, count, final, pool_branch, branch = pl.pallas_call(
        functools.partial(tables_kernel, (groups, blocks, held, pooled), pool_caps, caps),
        out_shape=tuple(jax.ShapeDtypeStruct((n,), jnp.int32) for n in sizes),
        in_specs=[SMEM, SMEM],
        out_specs=(SMEM,) * len(sizes),
        scratch_shapes=[pltpu.SMEM((n,), jnp.int32) for n in (blocks * held, chips, blocks * held, chips, blocks * held)],
        name="tables",
    )(where, routes_all)

    terms = lax.switch(
        pool_branch[0],
        [functools.partial(fetch, c, ("groups", "blk") if pooled else "blk", pooled, blocks) for c in pool_caps],
        where, src, pool, down_panels, up_panels, activations, out_grad, gates,
    )
    return lax.switch(
        branch[0],
        [functools.partial(give_back, c, blocks, held) for c in caps],
        where, slot, count, final, terms,
    )


def solution(mesh):
    in_specs = (
        P(("groups", "blk"), None),
        P(("groups", "blk"), None),
        P("blk", None, None),
        P("blk", None, None),
        P(("groups", "blk"), None),
        P(("groups", "blk"), None),
    )
    out_specs = (P(("groups", "blk"), None, None), P(("groups", "blk"), None, None))
    body = functools.partial(shards, mesh.shape["groups"], mesh.shape["blk"])
    return jax.shard_map(body, mesh=mesh, in_specs=in_specs, out_specs=out_specs, check_vma=False)
```

```python
import functools

import jax
import jax.numpy as jnp
from jax import lax
from jax.experimental import pallas as pl
from jax.experimental.pallas import tpu as pltpu
from jax.sharding import PartitionSpec as P

ANY = pl.BlockSpec(memory_space=pl.ANY)
HBM = pl.BlockSpec(memory_space=pltpu.HBM)
SMEM = pl.BlockSpec(memory_space=pltpu.SMEM)
VMEM = pl.BlockSpec(memory_space=pltpu.VMEM)
DMA = pltpu.SemaphoreType.DMA
BF16 = jnp.bfloat16
GROUP_CAPACITIES = (5, 6, 7, 8, 9, 10)
POOL_CAPACITIES = (9, 10, 11, 12, 13, 14, 15, 16)


def room_for(elements):
    return pltpu.CompilerParams(vmem_limit_bytes=2 * elements + (3 << 20))


def repeat(n, body, unroll=1):
    def step(i, carry):
        body(i)
        return carry

    lax.fori_loop(0, n, step, 0, unroll=unroll)


def branch_of(most, caps):
    return sum((most > c).astype(jnp.int32) for c in caps[:-1])


def tables_kernel(shape, pool_caps, caps, where_ref, routes_ref, src_ref, pool_ref, slot_ref, count_ref, final_ref, pool_branch_ref, branch_ref, pool_seen, pool_load, seen, load, origin):
    groups, blocks, held, pooled = shape
    requests = 2 * blocks
    chips = blocks // 2
    group, me = where_ref[0], where_ref[1]
    chip = lax.div(me, 2)
    zero = jnp.int32(0)

    def clear(ref, n, value):
        def body(i):
            ref[i] = value

        repeat(n, body, 8 if n % 8 == 0 else 4)

    def rank_of(seen, load, adapter, owner):
        before = seen[adapter]
        new = before < 0
        filled = load[owner]
        rank = jnp.where(new, filled, before)
        seen[adapter] = rank
        filled = filled + new.astype(jnp.int32)
        load[owner] = filled
        return rank, new, filled

    clear(src_ref, 2 * held, -1)
    clear(final_ref, held, -1)
    clear(pool_load, chips, 0)

    def scan(g, most, mine):
        clear(load, chips, 0)

        def unsee(b):
            for k in range(2):
                adapter = routes_ref[g * blocks + b, 0, k]
                seen[adapter] = -1

        repeat(blocks, unsee, 8)

        def visit(b, most):
            most, pool_most = most
            for k in range(2):
                i = 2 * b + k
                adapter = routes_ref[g * blocks + b, 0, k]
                owner = lax.div(adapter, 2 * held)
                rank, new, filled = rank_of(seen, load, adapter, owner)
                most = jnp.maximum(most, filled)
                if pooled:
                    pool_rank, _, filled = rank_of(pool_seen, pool_load, adapter, owner)
                    pool_most = jnp.maximum(pool_most, filled)
                    at = 2 * (g * requests + i)
                else:
                    pool_rank, at = rank, 2 * i
                if pooled or mine:
                    pool_ref[at] = owner
                    pool_ref[at + 1] = pool_rank
                    src_ref[jnp.where(owner == chip, pool_rank, 2 * held)] = adapter - owner * (2 * held)
                if mine:
                    slot_ref[2 * i] = owner
                    slot_ref[2 * i + 1] = rank
                    count_ref[i] = 0
                    start = jnp.where(new, i, origin[adapter])
                    origin[adapter] = start
                    count_ref[start] = count_ref[start] + 1
                    final_ref[jnp.where(lax.div(adapter, held) == me, adapter - me * held, held)] = rank
            return most, pool_most

        return lax.fori_loop(0, blocks, visit, most, unroll=4)

    if pooled:

        def unsee(b):
            for k in range(2):
                pool_seen[routes_ref[b, 0, k]] = -1

        repeat(groups * blocks, unsee, 8)
    most = scan(group, (zero, zero), True)
    most, pool_most = lax.fori_loop(0, groups - 1, lambda g, m: scan(jnp.where(g < group, g, g + 1), m, False), most)
    pool_branch_ref[0] = branch_of(pool_most if pooled else most, pool_caps)
    branch_ref[0] = branch_of(most, caps)


def take_slots(held, core, src_ref, cap, near, act):
    def visit(c):
        adapter = src_ref[c]

        @pl.when((adapter >= 0) & ((lax.div(adapter, held) == core) == near))
        def _():
            act(c, lax.rem(adapter, held))

    repeat(cap, visit)


def hand_over_kernel(cap, held, pooled, where_ref, src_ref, down_ref, up_ref, send_ref, keep_ref, sems):
    wide = send_ref.shape[2]
    core = lax.rem(where_ref[1], 2)
    columns = pl.ds(pl.multiple_of(where_ref[0] * wide, 128) if pooled else 0, wide)

    def each(do):
        for swap in range(2):

            @pl.when(core == swap)
            def _(swap=swap):
                kept, sent = (up_ref, down_ref) if swap else (down_ref, up_ref)

                def act(c, a):
                    do(pltpu.make_async_copy(sent.at[a, :, columns], send_ref.at[c], sems.at[c, 0]))
                    do(pltpu.make_async_copy(kept.at[a, :, columns], keep_ref.at[c], sems.at[c, 1]))

                take_slots(held, core, src_ref, cap, True, act)

    each(lambda copy: copy.start())
    each(lambda copy: copy.wait())


def cut_kernel(cap, held, chips, where_ref, src_ref, keep_ref, other_ref, out_ref):
    part = out_ref.shape[3]
    core = lax.rem(where_ref[1], 2)
    for near, ref in ((True, keep_ref), (False, other_ref)):

        def act(c, a, ref=ref):
            for p in range(chips):
                out_ref[p, c] = ref[c, :, p * part : (p + 1) * part]

        take_slots(held, core, src_ref, cap, near, act)


def pick_kernel(cap, pool_ref, held_ref, out_ref):
    def visit(i):
        out_ref[i] = held_ref[pool_ref[2 * i] * cap + pool_ref[2 * i + 1]]

    repeat(out_ref.shape[0], visit)


def terms_kernel(blocks, gates_ref, rows_ref, grads_ref, panels_ref, out_ref):
    devices, slots, rank, part = panels_ref.shape
    tokens = rows_ref.shape[0]
    last = (((1,), (1,)), ((), ()))

    def gather(s, sums):
        low, back = sums
        cols = pl.ds(pl.multiple_of(s * part, 128), part)
        down = panels_ref[2 * s].reshape(slots * rank, part)
        up = panels_ref[2 * s + 1].reshape(slots * rank, part)
        low += lax.dot_general(down, rows_ref[:, cols], last, preferred_element_type=jnp.float32)
        back += lax.dot_general(up, grads_ref[:, cols], last, preferred_element_type=jnp.float32)
        return low, back

    zero = jnp.zeros((slots * rank, tokens), jnp.float32)
    low, back = lax.fori_loop(0, devices // 2, gather, (zero, zero), unroll=8)
    low, back = low.astype(BF16), back.astype(BF16)
    wide = out_ref.shape[3]

    def spread(p, carry):
        cols = pl.ds(pl.multiple_of(p * wide, 128), wide)
        down = jnp.dot(back, rows_ref[:, cols], preferred_element_type=jnp.float32)
        up = jnp.dot(low, grads_ref[:, cols], preferred_element_type=jnp.float32)
        for k in range(slots):
            gate = gates_ref[0, k]
            out_ref[2 * p, k] = (down[k * rank : (k + 1) * rank] * gate).astype(out_ref.dtype)
            out_ref[2 * p + 1, k] = (up[k * rank : (k + 1) * rank] * gate).astype(out_ref.dtype)
        return carry

    lax.fori_loop(0, blocks // 2, spread, 0, unroll=8)


def merge_kernel(cap, slot_ref, count_ref, terms_ref, out_ref, total):
    requests = terms_ref.shape[0]

    def slot(i):
        return slot_ref[2 * i] * cap + slot_ref[2 * i + 1]

    def visit(i):
        @pl.when(count_ref[i] == 1)
        def _():
            out_ref[slot(i)] = terms_ref[i]

        @pl.when(count_ref[i] > 1)
        def _():
            s = slot(i)
            total[...] = terms_ref[i].astype(jnp.float32)

            def add(j, _):
                @pl.when(slot(j) == s)
                def _():
                    total[...] += terms_ref[j].astype(jnp.float32)

                return 0

            lax.fori_loop(i + 1, requests, add, 0)
            out_ref[s] = total[...].astype(out_ref.dtype)

    repeat(requests, visit, 4)


def zeros_kernel(down_ref, up_ref, zero, sems):
    held = down_ref.shape[0]
    zero[...] = jnp.zeros_like(zero)

    def each(act):
        def visit(a):
            act(pltpu.make_async_copy(zero, down_ref.at[a], sems.at[a, 0]))
            act(pltpu.make_async_copy(zero, up_ref.at[a], sems.at[a, 1]))

        repeat(held, visit)

    each(lambda copy: copy.start())
    each(lambda copy: copy.wait())


def home_kernel(chips, own, where_ref, final_ref, slices_ref, down_in_ref, up_in_ref, down_ref, up_ref, sems):
    held = down_ref.shape[0]
    part = slices_ref.shape[3]
    core = lax.rem(where_ref[1], 2)
    kind = core if own else 1 - core

    def each(do):
        def visit(a):
            slot = final_ref[a]
            for k, ref in ((0, down_ref), (1, up_ref)):

                @pl.when((slot >= 0) & (kind == k))
                def _(ref=ref):
                    for p in range(chips):
                        do(pltpu.make_async_copy(slices_ref.at[p, slot], ref.at[a, :, pl.ds(p * part, part)], sems.at[a, p]))

        repeat(held, visit)

    each(lambda copy: copy.start())
    each(lambda copy: copy.wait())


def fetch(cap, axes, pooled, blocks, where, src, pool, down_panels, up_panels, activations, out_grad, gates):
    held, rank, width = down_panels.shape
    chips = blocks // 2
    requests = pool.shape[0] // 2
    part = width // (chips * (requests // (2 * blocks)))
    same_core = [[2 * i + c for i in range(chips)] for c in range(2)]
    wide = part * chips
    panel = jax.ShapeDtypeStruct((cap, rank, wide), BF16)
    send, keep = pl.pallas_call(
        functools.partial(hand_over_kernel, cap, held, pooled),
        out_shape=(panel, panel),
        in_specs=[SMEM, SMEM, HBM, HBM],
        out_specs=(VMEM, VMEM),
        scratch_shapes=[DMA((cap, 2))],
        compiler_params=room_for(2 * cap * rank * wide),
        name="hand_over",
    )(where, src, down_panels, up_panels)
    other = lax.ppermute(send, "blk", [(i, i ^ 1) for i in range(blocks)])
    slices = pl.pallas_call(
        functools.partial(cut_kernel, cap, held, chips),
        out_shape=jax.ShapeDtypeStruct((chips, cap, rank, part), BF16),
        in_specs=[SMEM, SMEM, VMEM, VMEM],
        out_specs=VMEM,
        compiler_params=room_for(3 * cap * rank * wide),
        name="cut",
    )(where, src, keep, other)
    slices = lax.all_to_all(slices, "blk", 0, 0, tiled=True, axis_index_groups=same_core)
    picked = pl.pallas_call(
        functools.partial(pick_kernel, cap),
        out_shape=jax.ShapeDtypeStruct((requests, rank, part), BF16),
        in_specs=[SMEM, VMEM],
        out_specs=VMEM,
        compiler_params=room_for((chips * cap + requests) * rank * part),
        name="pick",
    )(pool, slices.reshape(chips * cap, rank, part))
    panels = lax.all_to_all(picked.reshape(requests // 2, 2, rank, part), axes, 0, 0, tiled=True)
    return pl.pallas_call(
        functools.partial(terms_kernel, blocks),
        out_shape=jax.ShapeDtypeStruct((blocks, 2, rank, width // chips), BF16),
        in_specs=[SMEM, VMEM, VMEM, VMEM],
        out_specs=VMEM,
        compiler_params=room_for(2 * out_grad.size + 2 * panels.size),
        name="terms",
    )(gates, activations, out_grad, panels)


def give_back(cap, blocks, held, where, slot, count, final, terms):
    _, _, rank, part = terms.shape
    chips = blocks // 2
    width = part * chips
    partner = [(i, i ^ 1) for i in range(blocks)]
    same_core = [[2 * i + c for i in range(chips)] for c in range(2)]
    terms = lax.all_to_all(terms, "blk", 0, 0, tiled=True)
    shape = jax.ShapeDtypeStruct((held, rank, width), BF16)
    grads = pl.pallas_call(
        zeros_kernel,
        out_shape=(shape, shape),
        in_specs=[],
        out_specs=(ANY, ANY),
        scratch_shapes=[pltpu.VMEM((rank, width), BF16), DMA((held, 2))],
        cost_estimate=pl.CostEstimate(flops=0, bytes_accessed=4 * held * rank * width, transcendentals=0),
        name="zeros",
    )()
    terms, grads = lax.optimization_barrier((terms, grads))
    sums = pl.pallas_call(
        functools.partial(merge_kernel, cap),
        out_shape=jax.ShapeDtypeStruct((chips * cap, rank, part), BF16),
        in_specs=[SMEM, SMEM, VMEM],
        out_specs=VMEM,
        scratch_shapes=[pltpu.VMEM((rank, part), jnp.float32)],
        compiler_params=room_for(terms.size + (chips * cap + 2) * rank * part),
        name="merge",
    )(slot, count, terms.reshape(2 * blocks, rank, part))
    own = lax.all_to_all(sums.reshape(chips, cap, rank, part), "blk", 0, 0, tiled=True, axis_index_groups=same_core)
    other = lax.ppermute(own, "blk", partner)
    for mine, slices in ((True, own), (False, other)):
        grads = pl.pallas_call(
            functools.partial(home_kernel, chips, mine),
            out_shape=(shape, shape),
            in_specs=[SMEM, SMEM, VMEM, ANY, ANY],
            out_specs=(ANY, ANY),
            scratch_shapes=[DMA((held, chips))],
            input_output_aliases={3: 0, 4: 1},
            cost_estimate=pl.CostEstimate(flops=0, bytes_accessed=4 * own.size, transcendentals=0),
            compiler_params=room_for(own.size),
            name="home_own" if mine else "home_other",
        )(where, final, slices, *grads)
    return grads


def shards(groups, blocks, activations, out_grad, down_panels, up_panels, routes, gates):
    held, rank, width = down_panels.shape
    chips = blocks // 2
    requests = 2 * blocks
    pooled = groups > 1 and width % (128 * chips * groups) == 0
    caps = [c for c in GROUP_CAPACITIES if c < 2 * held] + [2 * held]
    pool_caps = [c for c in POOL_CAPACITIES if c < 2 * held] + [2 * held] if pooled else caps

    where = jnp.stack([lax.axis_index("groups"), lax.axis_index("blk")]).astype(jnp.int32)
    copies = jnp.broadcast_to(routes.reshape(1, 1, 2), (groups * blocks, 1, 2))
    routes_all = lax.all_to_all(copies, ("groups", "blk"), 0, 0, tiled=True)
    sizes = (2 * held + 1, 2 * requests * (groups if pooled else 1), 2 * requests, requests, held + 1, 1, 1)
    src, pool, slot, count, final, pool_branch, branch = pl.pallas_call(
        functools.partial(tables_kernel, (groups, blocks, held, pooled), pool_caps, caps),
        out_shape=tuple(jax.ShapeDtypeStruct((n,), jnp.int32) for n in sizes),
        in_specs=[SMEM, SMEM],
        out_specs=(SMEM,) * len(sizes),
        scratch_shapes=[pltpu.SMEM((n,), jnp.int32) for n in (blocks * held, chips, blocks * held, chips, blocks * held)],
        name="tables",
    )(where, routes_all)

    terms = lax.switch(
        pool_branch[0],
        [functools.partial(fetch, c, ("groups", "blk") if pooled else "blk", pooled, blocks) for c in pool_caps],
        where, src, pool, down_panels, up_panels, activations, out_grad, gates,
    )
    return lax.switch(
        branch[0],
        [functools.partial(give_back, c, blocks, held) for c in caps],
        where, slot, count, final, terms,
    )


def solution(mesh):
    in_specs = (
        P(("groups", "blk"), None),
        P(("groups", "blk"), None),
        P("blk", None, None),
        P("blk", None, None),
        P(("groups", "blk"), None),
        P(("groups", "blk"), None),
    )
    out_specs = (P(("groups", "blk"), None, None), P(("groups", "blk"), None, None))
    body = functools.partial(shards, mesh.shape["groups"], mesh.shape["blk"])
    return jax.shard_map(body, mesh=mesh, in_specs=in_specs, out_specs=out_specs, check_vma=False)
```
